512 devices in a mesh: dp: 16 (over z_hi, x), row: 8 (over y, core), col: 4 (over z_lo).
Axes of the slice: x: 4, y: 4, z: 16 (z_hi: 4, z_lo: 4; z = z_hi * 4 + z_lo), core: 2. Of those that a mesh axis runs over, the one named last changes fastest.
Arguments:
- tokens: bfloat16 [4096, 4096], P('dp', 'col'), may hold values from -6 to 6
- cotangent: bfloat16 [4096, 4096], P('dp', 'col'), may hold values from -6 to 6
- counts: int32 [16], P('dp'), may hold values from 1 to 4, as said below
- up_blocks: bfloat16 [4, 8, 32, 128, 128], P('col', 'row'), may hold values from -0.1875 to 0.1875
- up_rows: int32 [4, 8, 32], P('col', 'row'), may hold values from 0 to 7, as said below
- up_cols: int32 [4, 8, 32], P('col', 'row'), may hold values from 0 to 15, as said below
- down_blocks: bfloat16 [8, 4, 32, 128, 128], P('row', 'col'), may hold values from -0.09375 to 0.09375
- down_rows: int32 [8, 4, 32], P('row', 'col'), may hold values from 0 to 15, as said below
- down_cols: int32 [8, 4, 32], P('row', 'col'), may hold values from 0 to 7, as said below
Outputs:
- y_out: bfloat16 [4096, 4096], P('dp', 'col')
- grad_tokens: bfloat16 [4096, 4096], P('dp', 'col')
- grad_up: float32 [4, 8, 32, 128, 128], P('col', 'row', 'dp')
- grad_down: float32 [8, 4, 32, 128, 128], P('row', 'col', 'dp')
The draws below stay inside these ranges and needn't reach their ends.
Inputs may be any that keep to these rules, and one draw needn't show every extreme that they name: Replica d has counts[d] live microbatches of 64 tokens in its first slots; the rest of its 4 slots are padding. `up_rows`: within each tile the 32 blocks stand at distinct positions, and every tile holds its block (0, 0) and its block (7, 15). `up_cols`: paired with up_rows as above. `down_rows`: within each tile the 32 blocks stand at distinct positions, and every tile holds its block (0, 0) and its block (15, 7). `down_cols`: paired with down_rows as above.
All inputs are finite; a program needn't handle non-finite values.
Results may differ from the reference program's by a relative error of at most 0.029.
Values may be sent and summed in bfloat16 or wider, within the bound.
A program may use at most 64 MiB of HBM per device.

```python
import jax
import jax.numpy as jnp
from jax import lax

D = 4096
FF = 16384
BLOCK = 128
MB_TOK = 64
MB_MAX = 4
CAP = 256
TOKENS = 4096
TILE_D = 8
TILE_F = 16
NB = 32
N_DP = 16
N_ROW = 8
N_COL = 4


def tile_pattern(key, tile_count, row_cells, col_cells, block_count):
    cell_count = row_cells * col_cells
    tile_keys = jax.random.split(key, tile_count)

    def one_tile(tile_key):
        first_key, second_key = jax.random.split(tile_key)
        middle = jax.random.permutation(first_key, cell_count - 2)[:block_count - 2].astype(jnp.int32) + 1
        chosen = jnp.concatenate([jnp.zeros((1,), jnp.int32), middle, jnp.full((1,), cell_count - 1, jnp.int32)])
        shuffle = jax.random.permutation(second_key, block_count)
        chosen = chosen[shuffle]
        return (chosen // col_cells, chosen % col_cells)
    return jax.vmap(one_tile)(tile_keys)


def draw_up_rows(key, part):
    block_rows, block_cols = tile_pattern(jax.random.fold_in(key, 11), N_COL * N_ROW, TILE_D, TILE_F, NB)
    return block_rows.reshape(N_COL, N_ROW, NB).astype(jnp.int32)


def draw_up_cols(key, part):
    block_rows, block_cols = tile_pattern(jax.random.fold_in(key, 11), N_COL * N_ROW, TILE_D, TILE_F, NB)
    return block_cols.reshape(N_COL, N_ROW, NB).astype(jnp.int32)


def draw_down_rows(key, part):
    block_rows, block_cols = tile_pattern(jax.random.fold_in(key, 23), N_ROW * N_COL, TILE_F, TILE_D, NB)
    return block_rows.reshape(N_ROW, N_COL, NB).astype(jnp.int32)


def draw_down_cols(key, part):
    block_rows, block_cols = tile_pattern(jax.random.fold_in(key, 23), N_ROW * N_COL, TILE_F, TILE_D, NB)
    return block_cols.reshape(N_ROW, N_COL, NB).astype(jnp.int32)


def draw_counts(key, part):
    key_one, key_two, key_three, key_four = jax.random.split(jax.random.fold_in(key, 37), 4)
    busy_flag = jax.random.randint(key_one, (N_DP,), 0, 4) == 0
    extra_count = jax.random.randint(key_two, (N_DP,), 2, MB_MAX + 1)
    micro_counts = jnp.where(busy_flag, extra_count, 1).astype(jnp.int32)
    top_index = jax.random.randint(key_three, (), 0, N_DP)
    low_index = (top_index + jax.random.randint(key_four, (), 1, N_DP)) % N_DP
    micro_counts = micro_counts.at[top_index].set(MB_MAX)
    micro_counts = micro_counts.at[low_index].set(1)
    return micro_counts


def block_scale(rng, extent, pieces, smallest, largest):
    loudness = 1.0
    for dim, parts in pieces:
        steps = jax.random.uniform(jax.random.fold_in(jax.random.fold_in(rng, 6), dim), (parts,), jnp.float32, smallest / len(pieces), largest / len(pieces))
        loudness = loudness * jnp.repeat(jnp.exp(steps), extent[dim] // parts).reshape((-1,) + (1,) * (len(extent) - 1 - dim))
    return loudness


def gaussian(key, dims, spread, limit, pieces=(), held_as=jnp.bfloat16):
    array = spread * jax.random.normal(key, dims, jnp.float32)
    if pieces:
        array = array * block_scale(key, dims, pieces, -0.22, 0.18)
    return jnp.clip(array, -limit, limit).astype(held_as)


def setup_inputs(seed: int = 0) -> dict:
    seeds = jax.random.split(jax.random.key(seed), 10)
    return {
        "tokens": gaussian(seeds[0], (TOKENS, D), 1.0, 6.0, ((0, 16), (1, 4))),
        "cotangent": gaussian(seeds[1], (TOKENS, D), 1.0, 6.0, ((0, 16), (1, 4))),
        "counts": draw_counts(jax.random.fold_in(seeds[9], 71), 0),
        "up_blocks": gaussian(seeds[3], (N_COL, N_ROW, NB, BLOCK, BLOCK), (D // 4) ** -0.5, 0.1875, ((0, 4), (1, 8))),
        "up_rows": draw_up_rows(jax.random.fold_in(seeds[9], 71), 0),
        "up_cols": draw_up_cols(jax.random.fold_in(seeds[9], 71), 0),
        "down_blocks": gaussian(seeds[6], (N_ROW, N_COL, NB, BLOCK, BLOCK), (FF // 4) ** -0.5, 0.09375, ((0, 8), (1, 4))),
        "down_rows": draw_down_rows(jax.random.fold_in(seeds[9], 71), 0),
        "down_cols": draw_down_cols(jax.random.fold_in(seeds[9], 71), 0),
    }


def wire_round(values):
    return lax.optimization_barrier(values.astype(jnp.bfloat16)).astype(jnp.float32)


def gelu_exact(hidden_in):
    return 0.5 * hidden_in * (1.0 + jax.scipy.special.erf(hidden_in * 0.7071067811865476))


def gelu_slope(hidden_in):
    normal_cdf = 0.5 * (1.0 + jax.scipy.special.erf(hidden_in * 0.7071067811865476))
    return normal_cdf + hidden_in * jnp.exp(-0.5 * hidden_in * hidden_in) * 0.3989422804014327


def tile_product(operand, blocks, in_index, out_index, out_count, flipped):
    row_count = operand.shape[0]
    selected = jnp.take(operand.reshape(row_count, -1, BLOCK), in_index, axis=1).astype(jnp.float32)
    pattern = "tnj,nkj->tnk" if flipped else "tnk,nkj->tnj"
    products = jnp.einsum(pattern, selected, blocks.astype(jnp.float32))
    placing = (out_index[:, None] == jnp.arange(out_count, dtype=jnp.int32)[None, :]).astype(jnp.float32)
    combined = jnp.einsum("tnj,nb->tbj", products, placing)
    return combined.reshape(row_count, out_count * BLOCK)


def block_terms(left_side, right_side, left_index, right_index):
    left_slab = jnp.take(left_side.reshape(TOKENS, -1, BLOCK), left_index, axis=1).astype(jnp.float32)
    right_slab = jnp.take(right_side.reshape(TOKENS, -1, BLOCK), right_index, axis=1).astype(jnp.float32)
    return jnp.einsum("tnk,tnj->nkj", left_slab, right_slab)


def reference(tokens, cotangent, counts, up_blocks, up_rows, up_cols, down_blocks, down_rows, down_cols):
    width_cols = TILE_D * BLOCK
    hidden_cols = TILE_F * BLOCK
    position = jnp.arange(TOKENS, dtype=jnp.int32)
    replica = position // CAP
    micro_slot = (position % CAP) // MB_TOK
    live_rows = (micro_slot < jnp.take(counts, replica)).astype(jnp.float32)[:, None]
    total_count = jnp.sum(counts).astype(jnp.float32)

    hidden_pieces = []
    for row_index in range(N_ROW):
        summed = jnp.zeros((TOKENS, hidden_cols), jnp.float32)
        for col_index in range(N_COL):
            operand = tokens[:, col_index * width_cols:(col_index + 1) * width_cols]
            summed = summed + wire_round(tile_product(operand, up_blocks[col_index, row_index], up_rows[col_index, row_index], up_cols[col_index, row_index], TILE_F, False))
        hidden_pieces.append(summed)
    hidden = jnp.concatenate(hidden_pieces, axis=1)
    activation = gelu_exact(hidden).astype(jnp.bfloat16)

    output_pieces = []
    for col_index in range(N_COL):
        summed = jnp.zeros((TOKENS, width_cols), jnp.float32)
        for row_index in range(N_ROW):
            operand = activation[:, row_index * hidden_cols:(row_index + 1) * hidden_cols]
            summed = summed + wire_round(tile_product(operand, down_blocks[row_index, col_index], down_rows[row_index, col_index], down_cols[row_index, col_index], TILE_D, False))
        output_pieces.append(summed)
    y_out = (jnp.concatenate(output_pieces, axis=1) * live_rows).astype(jnp.bfloat16)

    grad_mask = cotangent * live_rows.astype(jnp.bfloat16)
    act_pieces = []
    for row_index in range(N_ROW):
        summed = jnp.zeros((TOKENS, hidden_cols), jnp.float32)
        for col_index in range(N_COL):
            operand = grad_mask[:, col_index * width_cols:(col_index + 1) * width_cols]
            summed = summed + wire_round(tile_product(operand, down_blocks[row_index, col_index], down_cols[row_index, col_index], down_rows[row_index, col_index], TILE_F, True))
        act_pieces.append(summed)
    act_grad = jnp.concatenate(act_pieces, axis=1)
    hidden_grad = (act_grad * gelu_slope(hidden)).astype(jnp.bfloat16)

    input_pieces = []
    for col_index in range(N_COL):
        summed = jnp.zeros((TOKENS, width_cols), jnp.float32)
        for row_index in range(N_ROW):
            operand = hidden_grad[:, row_index * hidden_cols:(row_index + 1) * hidden_cols]
            summed = summed + wire_round(tile_product(operand, up_blocks[col_index, row_index], up_cols[col_index, row_index], up_rows[col_index, row_index], TILE_D, True))
        input_pieces.append(summed)
    grad_tokens = jnp.concatenate(input_pieces, axis=1).astype(jnp.bfloat16)

    up_list = []
    for col_index in range(N_COL):
        inner = []
        for row_index in range(N_ROW):
            left_side = tokens[:, col_index * width_cols:(col_index + 1) * width_cols]
            right_side = hidden_grad[:, row_index * hidden_cols:(row_index + 1) * hidden_cols]
            inner.append(block_terms(left_side, right_side, up_rows[col_index, row_index], up_cols[col_index, row_index]) / total_count)
        up_list.append(jnp.stack(inner))
    grad_up = jnp.stack(up_list)

    down_list = []
    for row_index in range(N_ROW):
        inner = []
        for col_index in range(N_COL):
            left_side = activation[:, row_index * hidden_cols:(row_index + 1) * hidden_cols]
            right_side = grad_mask[:, col_index * width_cols:(col_index + 1) * width_cols]
            inner.append(block_terms(left_side, right_side, down_rows[row_index, col_index], down_cols[row_index, col_index]) / total_count)
        down_list.append(jnp.stack(inner))
    grad_down = jnp.stack(down_list)
    return (y_out, grad_tokens, grad_up, grad_down)
```

```python
import jax
import jax.numpy as jnp
from jax import lax
from jax.experimental import pallas as pl
from jax.experimental.pallas import tpu as pltpu
from jax.sharding import PartitionSpec as P

MESH = pl.DeviceIdType.MESH
BF = jnp.bfloat16
F32 = jnp.float32
B = 128
CAP = 256
MB_TOK = 64
STEPS = 8
TD = 8
NB = 32
LAG = 4
CH = 2 * B + 16
QR = 32

NT = (((1,), (1,)), ((), ()))
NN = (((1,), (0,)), ((), ()))


def dot(a, b, dims=NN):
    return lax.dot_general(a, b, dims, preferred_element_type=F32)


def kernel(
    counts, inv_up, inv_down, up_rows, up_cols, down_rows, down_cols,
    tokens, cotangent, up_blocks, down_blocks,
    y_out, g_out, gu_out, gd_out,
    gm, tok_t, gm_t, wup, wdn, part, rbuf, ah, yacc, gacc,
    fs, fr, ys, yr, yo, gbuf, xr, zbuf, zr,
    rs_s, rs_r, ag_s, ag_r, f_s, f_r, y_s, y_r, ya_s, ya_r, sb_s, sb_r, x_s, x_r, z_s, z_r,
):
    c = lax.axis_index("col")
    row = lax.axis_index("row")
    dp = lax.axis_index("dp")
    core = row % 2
    yi = row // 2
    hi = dp // 4
    xi = dp % 4
    count = counts[0]

    sibling = {"row": row + 1 - 2 * core}
    y_right = {"row": (row + 2) % 8}
    y_left = {"row": (row + 6) % 8}
    x_right = {"dp": hi * 4 + (xi + 1) % 4}
    x_left = {"dp": hi * 4 + (xi + 3) % 4}
    z_right = {"dp": ((hi + 1) % 4) * 4 + xi}
    z_left = {"dp": ((hi + 3) % 4) * 4 + xi}

    def send(src, dst, s_sem, r_sem, device):
        return pltpu.make_async_remote_copy(
            src_ref=src, dst_ref=dst, send_sem=s_sem, recv_sem=r_sem,
            device_id=device, device_id_type=MESH,
        )

    barrier = pltpu.get_barrier_semaphore()
    for peer in (sibling, y_right, y_left, x_right, x_left, z_right, z_left):
        pl.semaphore_signal(barrier, inc=1, device_id=peer, device_id_type=MESH)

    @pl.when(c > 0)
    def _():
        pl.semaphore_signal(barrier, inc=1, device_id={"col": c - 1}, device_id_type=MESH)

    @pl.when(c < 3)
    def _():
        pl.semaphore_signal(barrier, inc=1, device_id={"col": c + 1}, device_id_type=MESH)

    live = (lax.broadcasted_iota(jnp.int32, (CAP, 1), 0) // MB_TOK < count).astype(F32)
    gm[...] = (cotangent[...].astype(F32) * live).astype(BF)

    inside = jnp.where((c > 0) & (c < 3), 1, 0)
    pl.semaphore_wait(barrier, 8 + inside)

    def place(s):
        q = c + s * (3 - 2 * c)
        return q, c + 1 - 2 * s, c - 1 + 2 * s

    def rs_copy(j, device):
        return send(rbuf.at[j], rbuf.at[j], rs_s.at[j], rs_r.at[j], {"col": device})

    def ag_copy(j, device):
        return send(ah.at[j], ah.at[j], ag_s.at[j], ag_r.at[j], {"col": device})

    def partials(k, carry):
        for s in range(2):
            for i in range(TD):
                iu = inv_up[i * 16 + k + 8 * s]
                blk = up_blocks[jnp.minimum(iu, NB - 1)]
                wup[k, i * B:(i + 1) * B, s * B:(s + 1) * B] = jnp.where(iu < NB, blk, jnp.zeros_like(blk))
                idn = inv_down[(k + 8 * s) * 8 + i]
                blk = down_blocks[jnp.minimum(idn, NB - 1)]
                wdn[k, s * B:(s + 1) * B, i * B:(i + 1) * B] = jnp.where(idn < NB, blk, jnp.zeros_like(blk))
        hp = dot(tokens[...], wup[k])
        ap = dot(gm[...], wdn[k], NT)
        for s in range(2):
            part[k + 8 * s, 0] = hp[:, s * B:(s + 1) * B]
            part[k + 8 * s, 1] = ap[:, s * B:(s + 1) * B]

        @pl.when(c == 0)
        def _():
            rbuf[k, 0] = hp[:, :B].astype(BF)
            rbuf[k, 1] = ap[:, :B].astype(BF)
            rs_copy(k, 1).start()

        @pl.when(c == 3)
        def _():
            rbuf[k + 8, 0] = hp[:, B:].astype(BF)
            rbuf[k + 8, 1] = ap[:, B:].astype(BF)
            rs_copy(k + 8, 2).start()

        return carry

    lax.fori_loop(0, STEPS, partials, 0)

    yacc[...] = jnp.zeros_like(yacc)
    gacc[...] = jnp.zeros_like(gacc)
    for i in range(TD):
        tok_t[i] = tokens[:, i * B:(i + 1) * B].T
        gm_t[i] = gm[:, i * B:(i + 1) * B].T

    first = c // 2

    def sum_step(k, s):
        q, nxt, prv = place(s)
        j = s * 8 + k

        @pl.when(q > 0)
        def _():
            rs_copy(j, nxt).wait_recv()

        @pl.when((q > 0) & (q < 3))
        def _():
            rbuf[j] = (rbuf[j].astype(F32) + part[j]).astype(BF)
            rs_copy(j, nxt).start()

        @pl.when(q == 3)
        def _():
            h = rbuf[j, 0].astype(F32) + part[j, 0]
            a = rbuf[j, 1].astype(F32) + part[j, 1]
            cdf = 0.5 * (1.0 + lax.erf(h * 0.7071067811865476))
            ah[j, 0] = (h * cdf).astype(BF)
            slope = cdf + h * jnp.exp(-0.5 * h * h) * 0.3989422804014327
            ah[j, 1] = (a * slope).astype(BF)
            ag_copy(j, prv).start()

    def share_step(k, s):
        q, nxt, prv = place(s)
        j = s * 8 + k

        @pl.when(q < 3)
        def _():
            ag_copy(j, prv).wait_recv()

        @pl.when((q > 0) & (q < 3))
        def _():
            ag_copy(j, prv).start()

    def use_step(k):
        act = jnp.concatenate([ah[k, 0], ah[k + 8, 0]], axis=1)
        yacc[...] += dot(act, wdn[k])
        hg = jnp.concatenate([ah[k, 1], ah[k + 8, 1]], axis=1)
        gacc[...] += dot(hg, wup[k], NT)

    def line(it, carry):
        @pl.when(it < STEPS)
        def _():
            sum_step(it, first)
            sum_step(it, 1 - first)

        @pl.when(it >= LAG)
        def _():
            share_step(it - LAG, 1 - first)
            share_step(it - LAG, first)
            use_step(it - LAG)

        return carry

    lax.fori_loop(0, STEPS + LAG, line, 0)

    mine = pl.multiple_of(core * B, B)
    other = pl.multiple_of((1 - core) * B, B)
    fs[0] = yacc[pl.ds(other, B), :].astype(BF)
    fs[1] = gacc[pl.ds(other, B), :].astype(BF)
    pair = send(fs, fr, f_s, f_r, sibling)
    pair.start()

    count_rows = jnp.zeros((16, B), F32) + count.astype(F32)

    def grads(t, zh):
        def body(xq, carry):
            for b in range(2):
                k = (zh * 4 + xq) * 2 + b
                gu = dot(tok_t[up_rows[k]], ah[up_cols[k], 1])
                gbuf[0, t, xq, b * B:(b + 1) * B, :] = gu.astype(BF)
                gd = dot(gm_t[down_cols[k]], ah[down_rows[k], 0])
                gbuf[1, t, xq, b * B:(b + 1) * B, :] = gd.astype(BF)
            gbuf[0, t, xq, 2 * B:, :] = count_rows.astype(BF)
            gbuf[1, t, xq, 2 * B:, :] = count_rows.astype(BF)
            return carry

        lax.fori_loop(0, 4, body, 0)

    order = [(hi + 2) % 4, (hi + 1) % 4, (hi + 3) % 4, hi]
    x1, x2, x3 = (xi + 1) % 4, (xi + 2) % 4, (xi + 3) % 4

    def x_msg(t, m):
        src = (
            gbuf.at[0, t, x2], gbuf.at[1, t, x2], gbuf.at[1, t, x1], gbuf.at[0, t, x3],
            xr.at[t, 0], xr.at[t, 1],
        )[m]
        return send(src, xr.at[t, m], x_s.at[t, m], x_r.at[t, m], x_left if m % 2 else x_right)

    def x_start(t):
        for m in range(4):
            x_msg(t, m).start()

    def x_relay(t):
        x_msg(t, 0).wait_recv()
        xr[t, 0] = (xr[t, 0].astype(F32) + gbuf[0, t, x1].astype(F32)).astype(BF)
        x_msg(t, 4).start()
        x_msg(t, 1).wait_recv()
        xr[t, 1] = (xr[t, 1].astype(F32) + gbuf[1, t, x3].astype(F32)).astype(BF)
        x_msg(t, 5).start()

    def x_final(t):
        for m in range(2, 6):
            x_msg(t, m).wait_recv()
        zbuf[0, t] = (gbuf[0, t, xi].astype(F32) + xr[t, 3].astype(F32) + xr[t, 4].astype(F32)).astype(BF)
        zbuf[1, t] = (gbuf[1, t, xi].astype(F32) + xr[t, 2].astype(F32) + xr[t, 5].astype(F32)).astype(BF)

    def z_msg(m):
        src = (zbuf.at[0, 0], zbuf.at[1, 0], zbuf.at[1, 1], zbuf.at[0, 2], zr.at[0], zr.at[1])[m]
        return send(src, zr.at[m], z_s.at[m], z_r.at[m], z_left if m % 2 else z_right)

    def y_msg(m):
        src = (ys.at[0], ys.at[1], ys.at[2], ys.at[3], yr.at[0], yr.at[1])[m]
        return send(src, yr.at[m], y_s.at[m], y_r.at[m], y_left if m % 2 else y_right)

    def rows_of(acc, chunk):
        return acc[pl.ds(pl.multiple_of(core * B + chunk * QR, QR), QR), :]

    y1, y2, y3 = (yi + 1) % 4, (yi + 2) % 4, (yi + 3) % 4

    def y_share(m):
        g0 = core * 4 + yi
        if m < 2:
            ref = yo.at[g0]
        elif m == 2:
            ref = yo.at[core * 4 + y3, 0]
        else:
            ref = yo.at[core * 4 + y1, 1]
        return send(ref, ref, ya_s.at[m], ya_r.at[m], y_left if m % 2 else y_right)

    def y_arrived(m):
        if m == 0:
            ref = yo.at[core * 4 + y3]
        elif m == 1:
            ref = yo.at[core * 4 + y1]
        else:
            ref = yo.at[core * 4 + y2, m - 2]
        return send(ref, ref, ya_s.at[m], ya_r.at[m], y_left if m % 2 else y_right)

    def twin(m, half):
        ref = yo.at[half * 4 + (yi, y3, y1, y2)[m]]
        return send(ref, ref, sb_s.at[m], sb_r.at[m], sibling)

    grads(0, order[0])
    x_start(0)

    pair.wait_recv()
    yacc[pl.ds(mine, B), :] += fr[0].astype(F32)
    gacc[pl.ds(mine, B), :] += fr[1].astype(F32)
    ys[0] = rows_of(yacc, y2).astype(BF)
    ys[1] = rows_of(gacc, y2).astype(BF)
    ys[2] = rows_of(gacc, y1).astype(BF)
    ys[3] = rows_of(yacc, y3).astype(BF)
    for m in range(4):
        y_msg(m).start()

    grads(1, order[1])
    x_start(1)
    x_relay(0)

    y_msg(0).wait_recv()
    yr[0] = (yr[0].astype(F32) + rows_of(yacc, y1)).astype(BF)
    y_msg(4).start()
    y_msg(1).wait_recv()
    yr[1] = (yr[1].astype(F32) + rows_of(gacc, y3)).astype(BF)
    y_msg(5).start()

    grads(2, order[2])
    x_start(2)
    x_relay(1)
    x_final(0)
    z_msg(0).start()
    z_msg(1).start()

    for m in range(2, 6):
        y_msg(m).wait_recv()
    live_chunk = (core * 2 + yi // 2 < count).astype(F32)
    y_sum = rows_of(yacc, yi) + yr[3].astype(F32) + yr[4].astype(F32)
    yo[core * 4 + yi, 0] = (y_sum * live_chunk).astype(BF)
    yo[core * 4 + yi, 1] = (rows_of(gacc, yi) + yr[2].astype(F32) + yr[5].astype(F32)).astype(BF)
    y_share(0).start()
    y_share(1).start()
    twin(0, core).start()

    grads(3, order[3])
    x_start(3)
    x_relay(2)
    x_final(1)
    z_msg(2).start()

    y_arrived(0).wait_recv()
    y_share(2).start()
    twin(1, core).start()
    y_arrived(1).wait_recv()
    y_share(3).start()
    twin(2, core).start()

    z_msg(0).wait_recv()
    zr[0] = (zr[0].astype(F32) + zbuf[0, 1].astype(F32)).astype(BF)
    z_msg(4).start()

    x_relay(3)
    x_final(2)
    z_msg(3).start()
    z_msg(1).wait_recv()
    zr[1] = (zr[1].astype(F32) + zbuf[1, 2].astype(F32)).astype(BF)
    z_msg(5).start()

    y_arrived(2).wait_recv()
    y_arrived(3).wait_recv()
    twin(3, core).start()

    x_final(3)
    for m in range(4):
        twin(m, 1 - core).wait_recv()
    for half in range(2):
        for chunk in range(4):
            at = half * B + chunk * QR
            y_out[at:at + QR, :] = yo[half * 4 + chunk, 0]
            g_out[at:at + QR, :] = yo[half * 4 + chunk, 1]

    for m in range(2, 6):
        z_msg(m).wait_recv()
    gu_sum = zbuf[0, 3].astype(F32) + zr[3].astype(F32) + zr[4].astype(F32)
    gd_sum = zbuf[1, 3].astype(F32) + zr[2].astype(F32) + zr[5].astype(F32)
    total = gu_sum[2 * B:2 * B + 1, :]
    for b in range(2):
        gu_out[b] = gu_sum[b * B:(b + 1) * B, :] / total
        gd_out[b] = (gd_sum[b * B:(b + 1) * B, :] / total).T

    for s in range(2):
        q, nxt, prv = place(s)

        @pl.when(q < 3)
        def _(s=s, nxt=nxt):
            lax.fori_loop(0, STEPS, lambda k, v: (rs_copy(s * 8 + k, nxt).wait_send(), v)[1], 0)

        @pl.when(q > 0)
        def _(s=s, prv=prv):
            lax.fori_loop(0, STEPS, lambda k, v: (ag_copy(s * 8 + k, prv).wait_send(), v)[1], 0)

    pair.wait_send()
    for m in range(6):
        y_msg(m).wait_send()
        z_msg(m).wait_send()
        for t in range(4):
            x_msg(t, m).wait_send()
    for m in range(4):
        y_share(m).wait_send()
        twin(m, core).wait_send()


def inverse(position):
    slots = jnp.arange(B, dtype=jnp.int32)
    order = jnp.arange(NB, dtype=jnp.int32)
    hit = position[None, :] == slots[:, None]
    return NB - jnp.sum(jnp.where(hit, NB - order[None, :], 0), axis=1).astype(jnp.int32)


def body(tokens, cotangent, counts, up_blocks, up_rows, up_cols, down_blocks, down_rows, down_cols):
    ur, uc = up_rows[0, 0], up_cols[0, 0]
    dr, dc = down_rows[0, 0], down_cols[0, 0]
    inv_up = inverse(ur * 16 + uc)
    inv_down = inverse(dr * 8 + dc)
    smem = pl.BlockSpec(memory_space=pltpu.SMEM)
    vmem = pl.BlockSpec(memory_space=pltpu.VMEM)
    width = TD * B
    dma = pltpu.SemaphoreType.DMA
    y_out, g_out, gu, gd = pl.pallas_call(
        kernel,
        out_shape=(
            jax.ShapeDtypeStruct((CAP, width), BF),
            jax.ShapeDtypeStruct((CAP, width), BF),
            jax.ShapeDtypeStruct((2, B, B), F32),
            jax.ShapeDtypeStruct((2, B, B), F32),
        ),
        in_specs=[smem] * 7 + [vmem] * 4,
        out_specs=(vmem,) * 4,
        scratch_shapes=[
            pltpu.VMEM((CAP, width), BF),
            pltpu.VMEM((TD, B, CAP), BF),
            pltpu.VMEM((TD, B, CAP), BF),
            pltpu.VMEM((STEPS, width, 2 * B), BF),
            pltpu.VMEM((STEPS, 2 * B, width), BF),
            pltpu.VMEM((16, 2, CAP, B), F32),
            pltpu.VMEM((16, 2, CAP, B), BF),
            pltpu.VMEM((16, 2, CAP, B), BF),
            pltpu.VMEM((CAP, width), F32),
            pltpu.VMEM((CAP, width), F32),
            pltpu.VMEM((2, B, width), BF),
            pltpu.VMEM((2, B, width), BF),
            pltpu.VMEM((4, QR, width), BF),
            pltpu.VMEM((6, QR, width), BF),
            pltpu.VMEM((8, 2, QR, width), BF),
            pltpu.VMEM((2, 4, 4, CH, B), BF),
            pltpu.VMEM((4, 6, CH, B), BF),
            pltpu.VMEM((2, 4, CH, B), BF),
            pltpu.VMEM((6, CH, B), BF),
            dma((16,)), dma((16,)), dma((16,)), dma((16,)),
            dma, dma, dma((6,)), dma((6,)), dma((4,)), dma((4,)), dma((4,)), dma((4,)),
            dma((4, 6)), dma((4, 6)), dma((6,)), dma((6,)),
        ],
        compiler_params=pltpu.CompilerParams(
            collective_id=0, has_side_effects=True, vmem_limit_bytes=56 << 20
        ),
    )(counts, inv_up, inv_down, ur, uc, dr, dc, tokens, cotangent, up_blocks[0, 0], down_blocks[0, 0])
    return y_out, g_out, gu[None, None], gd[None, None]


def solution(mesh):
    return jax.shard_map(
        body,
        mesh=mesh,
        in_specs=(
            P("dp", "col"),
            P("dp", "col"),
            P("dp"),
            P("col", "row", None, None, None),
            P("col", "row", None),
            P("col", "row", None),
            P("row", "col", None, None, None),
            P("row", "col", None),
            P("row", "col", None),
        ),
        out_specs=(
            P("dp", "col"),
            P("dp", "col"),
            P("col", "row", "dp", None, None),
            P("row", "col", "dp", None, None),
        ),
        check_vma=False,
    )
```

```python
import jax
import jax.numpy as jnp
from jax import lax
from jax.experimental import pallas as pl
from jax.experimental.pallas import tpu as pltpu
from jax.sharding import PartitionSpec as P

MESH = pl.DeviceIdType.MESH
BF = jnp.bfloat16
F32 = jnp.float32
B = 128
CAP = 256
MB_TOK = 64
STEPS = 8
TD = 8
NB = 32
LATE, NEAR, FAR = 2, 7, 9
CH = 2 * B + 16
QR = 32

NT = (((1,), (1,)), ((), ()))
NN = (((1,), (0,)), ((), ()))


def dot(a, b, dims=NN):
    return lax.dot_general(a, b, dims, preferred_element_type=F32)


def kernel(
    counts, inv_up, inv_down, up_rows, up_cols, down_rows, down_cols,
    tokens, cotangent, up_blocks, down_blocks,
    y_out, g_out, gu_out, gd_out,
    gm, tok_t, gm_t, wup, wdn, part, rbuf, ah, yacc, gacc,
    fs, fr, ys, yr, yo, gbuf, xr, zbuf, zr,
    rs_s, rs_r, ag_s, ag_r, f_s, f_r, y_s, y_r, ya_s, ya_r, sb_s, sb_r, x_s, x_r, z_s, z_r,
):
    c = lax.axis_index("col")
    row = lax.axis_index("row")
    dp = lax.axis_index("dp")
    core = row % 2
    yi = row // 2
    hi = dp // 4
    xi = dp % 4
    count = counts[0]

    sibling = {"row": row + 1 - 2 * core}
    y_right = {"row": (row + 2) % 8}
    y_left = {"row": (row + 6) % 8}
    x_right = {"dp": hi * 4 + (xi + 1) % 4}
    x_left = {"dp": hi * 4 + (xi + 3) % 4}
    z_right = {"dp": ((hi + 1) % 4) * 4 + xi}
    z_left = {"dp": ((hi + 3) % 4) * 4 + xi}

    def send(src, dst, s_sem, r_sem, device):
        return pltpu.make_async_remote_copy(
            src_ref=src, dst_ref=dst, send_sem=s_sem, recv_sem=r_sem,
            device_id=device, device_id_type=MESH,
        )

    barrier = pltpu.get_barrier_semaphore()
    for peer in (sibling, y_right, y_left, x_right, x_left, z_right, z_left):
        pl.semaphore_signal(barrier, inc=1, device_id=peer, device_id_type=MESH)

    @pl.when(c > 0)
    def _():
        pl.semaphore_signal(barrier, inc=1, device_id={"col": c - 1}, device_id_type=MESH)

    @pl.when(c < 3)
    def _():
        pl.semaphore_signal(barrier, inc=1, device_id={"col": c + 1}, device_id_type=MESH)

    live = (lax.broadcasted_iota(jnp.int32, (CAP, 1), 0) // MB_TOK < count).astype(F32)
    gm[...] = (cotangent[...].astype(F32) * live).astype(BF)

    inside = jnp.where((c > 0) & (c < 3), 1, 0)
    pl.semaphore_wait(barrier, 8 + inside)

    def place(s):
        q = c + s * (3 - 2 * c)
        return q, c + 1 - 2 * s, c - 1 + 2 * s

    def rs_copy(j, device):
        return send(rbuf.at[j], rbuf.at[j], rs_s.at[j], rs_r.at[j], {"col": device})

    def ag_copy(j, device):
        return send(ah.at[j], ah.at[j], ag_s.at[j], ag_r.at[j], {"col": device})

    def partials(k, carry):
        for s in range(2):
            for i in range(TD):
                iu = inv_up[i * 16 + k + 8 * s]
                blk = up_blocks[jnp.minimum(iu, NB - 1)]
                wup[k, i * B:(i + 1) * B, s * B:(s + 1) * B] = jnp.where(iu < NB, blk, jnp.zeros_like(blk))
                idn = inv_down[(k + 8 * s) * 8 + i]
                blk = down_blocks[jnp.minimum(idn, NB - 1)]
                wdn[k, s * B:(s + 1) * B, i * B:(i + 1) * B] = jnp.where(idn < NB, blk, jnp.zeros_like(blk))
        hp = dot(tokens[...], wup[k])
        ap = dot(gm[...], wdn[k], NT)
        for s in range(2):
            part[k + 8 * s, 0] = hp[:, s * B:(s + 1) * B]
            part[k + 8 * s, 1] = ap[:, s * B:(s + 1) * B]

        @pl.when(c == 0)
        def _():
            rbuf[k, 0] = hp[:, :B].astype(BF)
            rbuf[k, 1] = ap[:, :B].astype(BF)
            rs_copy(k, 1).start()

        @pl.when(c == 3)
        def _():
            rbuf[k + 8, 0] = hp[:, B:].astype(BF)
            rbuf[k + 8, 1] = ap[:, B:].astype(BF)
            rs_copy(k + 8, 2).start()

        return carry

    lax.fori_loop(0, STEPS, partials, 0)

    yacc[...] = jnp.zeros_like(yacc)
    gacc[...] = jnp.zeros_like(gacc)
    for i in range(TD):
        tok_t[i] = tokens[:, i * B:(i + 1) * B].T
        gm_t[i] = gm[:, i * B:(i + 1) * B].T

    first = c // 2

    def sum_step(k, s):
        q, nxt, prv = place(s)
        j = s * 8 + k

        @pl.when(q > 0)
        def _():
            rs_copy(j, nxt).wait_recv()

        @pl.when((q > 0) & (q < 3))
        def _():
            rbuf[j] = (rbuf[j].astype(F32) + part[j]).astype(BF)
            rs_copy(j, nxt).start()

        @pl.when(q == 3)
        def _():
            h = rbuf[j, 0].astype(F32) + part[j, 0]
            a = rbuf[j, 1].astype(F32) + part[j, 1]
            cdf = 0.5 * (1.0 + lax.erf(h * 0.7071067811865476))
            ah[j, 0] = (h * cdf).astype(BF)
            slope = cdf + h * jnp.exp(-0.5 * h * h) * 0.3989422804014327
            ah[j, 1] = (a * slope).astype(BF)
            ag_copy(j, prv).start()

    def share_step(k, s):
        q, nxt, prv = place(s)
        j = s * 8 + k

        @pl.when(q < 3)
        def _():
            ag_copy(j, prv).wait_recv()

        @pl.when((q > 0) & (q < 3))
        def _():
            ag_copy(j, prv).start()

    def use_step(k):
        act = jnp.concatenate([ah[k, 0], ah[k + 8, 0]], axis=1)
        yacc[...] += dot(act, wdn[k])
        hg = jnp.concatenate([ah[k, 1], ah[k + 8, 1]], axis=1)
        gacc[...] += dot(hg, wup[k], NT)

    def line(it, carry):
        def during(lag, step):
            pl.when((it >= lag) & (it < lag + STEPS))(lambda: step(it - lag))

        during(0, lambda k: sum_step(k, first))
        during(LATE, lambda k: sum_step(k, 1 - first))
        during(NEAR, lambda k: share_step(k, 1 - first))

        def last(k):
            share_step(k, first)
            use_step(k)

        during(FAR, last)
        return carry

    lax.fori_loop(0, STEPS + FAR, line, 0)

    mine = pl.multiple_of(core * B, B)
    other = pl.multiple_of((1 - core) * B, B)
    fs[0] = yacc[pl.ds(other, B), :].astype(BF)
    fs[1] = gacc[pl.ds(other, B), :].astype(BF)
    pair = send(fs, fr, f_s, f_r, sibling)
    pair.start()

    count_rows = jnp.zeros((16, B), F32) + count.astype(F32)

    def grads(t, zh):
        def body(xq, carry):
            for b in range(2):
                k = (zh * 4 + xq) * 2 + b
                gu = dot(tok_t[up_rows[k]], ah[up_cols[k], 1])
                gbuf[0, t, xq, b * B:(b + 1) * B, :] = gu.astype(BF)
                gd = dot(gm_t[down_cols[k]], ah[down_rows[k], 0])
                gbuf[1, t, xq, b * B:(b + 1) * B, :] = gd.astype(BF)
            gbuf[0, t, xq, 2 * B:, :] = count_rows.astype(BF)
            gbuf[1, t, xq, 2 * B:, :] = count_rows.astype(BF)
            return carry

        lax.fori_loop(0, 4, body, 0)

    order = [(hi + 2) % 4, (hi + 1) % 4, (hi + 3) % 4, hi]
    x1, x2, x3 = (xi + 1) % 4, (xi + 2) % 4, (xi + 3) % 4

    def x_msg(t, m):
        src = (
            gbuf.at[0, t, x2], gbuf.at[1, t, x2], gbuf.at[1, t, x1], gbuf.at[0, t, x3],
            xr.at[t, 0], xr.at[t, 1],
        )[m]
        return send(src, xr.at[t, m], x_s.at[t, m], x_r.at[t, m], x_left if m % 2 else x_right)

    def x_start(t):
        for m in range(4):
            x_msg(t, m).start()

    def x_relay(t):
        x_msg(t, 0).wait_recv()
        xr[t, 0] = (xr[t, 0].astype(F32) + gbuf[0, t, x1].astype(F32)).astype(BF)
        x_msg(t, 4).start()
        x_msg(t, 1).wait_recv()
        xr[t, 1] = (xr[t, 1].astype(F32) + gbuf[1, t, x3].astype(F32)).astype(BF)
        x_msg(t, 5).start()

    def x_final(t):
        for m in range(2, 6):
            x_msg(t, m).wait_recv()
        zbuf[0, t] = (gbuf[0, t, xi].astype(F32) + xr[t, 3].astype(F32) + xr[t, 4].astype(F32)).astype(BF)
        zbuf[1, t] = (gbuf[1, t, xi].astype(F32) + xr[t, 2].astype(F32) + xr[t, 5].astype(F32)).astype(BF)

    def z_msg(m):
        src = (zbuf.at[0, 0], zbuf.at[1, 0], zbuf.at[1, 1], zbuf.at[0, 2], zr.at[0], zr.at[1])[m]
        return send(src, zr.at[m], z_s.at[m], z_r.at[m], z_left if m % 2 else z_right)

    def y_msg(m):
        src = (ys.at[0], ys.at[1], ys.at[2], ys.at[3], yr.at[0], yr.at[1])[m]
        return send(src, yr.at[m], y_s.at[m], y_r.at[m], y_left if m % 2 else y_right)

    def rows_of(acc, chunk):
        return acc[pl.ds(pl.multiple_of(core * B + chunk * QR, QR), QR), :]

    y1, y2, y3 = (yi + 1) % 4, (yi + 2) % 4, (yi + 3) % 4

    def y_share(m):
        g0 = core * 4 + yi
        if m < 2:
            ref = yo.at[g0]
        elif m == 2:
            ref = yo.at[core * 4 + y3, 0]
        else:
            ref = yo.at[core * 4 + y1, 1]
        return send(ref, ref, ya_s.at[m], ya_r.at[m], y_left if m % 2 else y_right)

    def y_arrived(m):
        if m == 0:
            ref = yo.at[core * 4 + y3]
        elif m == 1:
            ref = yo.at[core * 4 + y1]
        else:
            ref = yo.at[core * 4 + y2, m - 2]
        return send(ref, ref, ya_s.at[m], ya_r.at[m], y_left if m % 2 else y_right)

    def twin(m, half):
        ref = yo.at[half * 4 + (yi, y3, y1, y2)[m]]
        return send(ref, ref, sb_s.at[m], sb_r.at[m], sibling)

    grads(0, order[0])
    x_start(0)

    pair.wait_recv()
    yacc[pl.ds(mine, B), :] += fr[0].astype(F32)
    gacc[pl.ds(mine, B), :] += fr[1].astype(F32)
    ys[0] = rows_of(yacc, y2).astype(BF)
    ys[1] = rows_of(gacc, y2).astype(BF)
    ys[2] = rows_of(gacc, y1).astype(BF)
    ys[3] = rows_of(yacc, y3).astype(BF)
    for m in range(4):
        y_msg(m).start()

    grads(1, order[1])
    x_start(1)
    x_relay(0)

    y_msg(0).wait_recv()
    yr[0] = (yr[0].astype(F32) + rows_of(yacc, y1)).astype(BF)
    y_msg(4).start()
    y_msg(1).wait_recv()
    yr[1] = (yr[1].astype(F32) + rows_of(gacc, y3)).astype(BF)
    y_msg(5).start()

    grads(2, order[2])
    x_start(2)
    x_relay(1)
    x_final(0)
    z_msg(0).start()
    z_msg(1).start()

    for m in range(2, 6):
        y_msg(m).wait_recv()
    live_chunk = (core * 2 + yi // 2 < count).astype(F32)
    y_sum = rows_of(yacc, yi) + yr[3].astype(F32) + yr[4].astype(F32)
    yo[core * 4 + yi, 0] = (y_sum * live_chunk).astype(BF)
    yo[core * 4 + yi, 1] = (rows_of(gacc, yi) + yr[2].astype(F32) + yr[5].astype(F32)).astype(BF)
    y_share(0).start()
    y_share(1).start()
    twin(0, core).start()

    grads(3, order[3])
    x_start(3)
    x_relay(2)
    x_final(1)
    z_msg(2).start()

    y_arrived(0).wait_recv()
    y_share(2).start()
    twin(1, core).start()
    y_arrived(1).wait_recv()
    y_share(3).start()
    twin(2, core).start()

    z_msg(0).wait_recv()
    zr[0] = (zr[0].astype(F32) + zbuf[0, 1].astype(F32)).astype(BF)
    z_msg(4).start()

    x_relay(3)
    x_final(2)
    z_msg(3).start()
    z_msg(1).wait_recv()
    zr[1] = (zr[1].astype(F32) + zbuf[1, 2].astype(F32)).astype(BF)
    z_msg(5).start()

    y_arrived(2).wait_recv()
    y_arrived(3).wait_recv()
    twin(3, core).start()

    x_final(3)
    for m in range(4):
        twin(m, 1 - core).wait_recv()
    for half in range(2):
        for chunk in range(4):
            at = half * B + chunk * QR
            y_out[at:at + QR, :] = yo[half * 4 + chunk, 0]
            g_out[at:at + QR, :] = yo[half * 4 + chunk, 1]

    for m in range(2, 6):
        z_msg(m).wait_recv()
    gu_sum = zbuf[0, 3].astype(F32) + zr[3].astype(F32) + zr[4].astype(F32)
    gd_sum = zbuf[1, 3].astype(F32) + zr[2].astype(F32) + zr[5].astype(F32)
    total = gu_sum[2 * B:2 * B + 1, :]
    for b in range(2):
        gu_out[b] = gu_sum[b * B:(b + 1) * B, :] / total
        gd_out[b] = (gd_sum[b * B:(b + 1) * B, :] / total).T

    for s in range(2):
        q, nxt, prv = place(s)

        @pl.when(q < 3)
        def _(s=s, nxt=nxt):
            lax.fori_loop(0, STEPS, lambda k, v: (rs_copy(s * 8 + k, nxt).wait_send(), v)[1], 0)

        @pl.when(q > 0)
        def _(s=s, prv=prv):
            lax.fori_loop(0, STEPS, lambda k, v: (ag_copy(s * 8 + k, prv).wait_send(), v)[1], 0)

    pair.wait_send()
    for m in range(6):
        y_msg(m).wait_send()
        z_msg(m).wait_send()
        for t in range(4):
            x_msg(t, m).wait_send()
    for m in range(4):
        y_share(m).wait_send()
        twin(m, core).wait_send()


def inverse(position):
    slots = jnp.arange(B, dtype=jnp.int32)
    order = jnp.arange(NB, dtype=jnp.int32)
    hit = position[None, :] == slots[:, None]
    return NB - jnp.sum(jnp.where(hit, NB - order[None, :], 0), axis=1).astype(jnp.int32)


def body(tokens, cotangent, counts, up_blocks, up_rows, up_cols, down_blocks, down_rows, down_cols):
    ur, uc = up_rows[0, 0], up_cols[0, 0]
    dr, dc = down_rows[0, 0], down_cols[0, 0]
    inv_up = inverse(ur * 16 + uc)
    inv_down = inverse(dr * 8 + dc)
    smem = pl.BlockSpec(memory_space=pltpu.SMEM)
    vmem = pl.BlockSpec(memory_space=pltpu.VMEM)
    width = TD * B
    dma = pltpu.SemaphoreType.DMA
    y_out, g_out, gu, gd = pl.pallas_call(
        kernel,
        out_shape=(
            jax.ShapeDtypeStruct((CAP, width), BF),
            jax.ShapeDtypeStruct((CAP, width), BF),
            jax.ShapeDtypeStruct((2, B, B), F32),
            jax.ShapeDtypeStruct((2, B, B), F32),
        ),
        in_specs=[smem] * 7 + [vmem] * 4,
        out_specs=(vmem,) * 4,
        scratch_shapes=[
            pltpu.VMEM((CAP, width), BF),
            pltpu.VMEM((TD, B, CAP), BF),
            pltpu.VMEM((TD, B, CAP), BF),
            pltpu.VMEM((STEPS, width, 2 * B), BF),
            pltpu.VMEM((STEPS, 2 * B, width), BF),
            pltpu.VMEM((16, 2, CAP, B), F32),
            pltpu.VMEM((16, 2, CAP, B), BF),
            pltpu.VMEM((16, 2, CAP, B), BF),
            pltpu.VMEM((CAP, width), F32),
            pltpu.VMEM((CAP, width), F32),
            pltpu.VMEM((2, B, width), BF),
            pltpu.VMEM((2, B, width), BF),
            pltpu.VMEM((4, QR, width), BF),
            pltpu.VMEM((6, QR, width), BF),
            pltpu.VMEM((8, 2, QR, width), BF),
            pltpu.VMEM((2, 4, 4, CH, B), BF),
            pltpu.VMEM((4, 6, CH, B), BF),
            pltpu.VMEM((2, 4, CH, B), BF),
            pltpu.VMEM((6, CH, B), BF),
            dma((16,)), dma((16,)), dma((16,)), dma((16,)),
            dma, dma, dma((6,)), dma((6,)), dma((4,)), dma((4,)), dma((4,)), dma((4,)),
            dma((4, 6)), dma((4, 6)), dma((6,)), dma((6,)),
        ],
        compiler_params=pltpu.CompilerParams(
            collective_id=0, has_side_effects=True, vmem_limit_bytes=56 << 20
        ),
    )(counts, inv_up, inv_down, ur, uc, dr, dc, tokens, cotangent, up_blocks[0, 0], down_blocks[0, 0])
    return y_out, g_out, gu[None, None], gd[None, None]


def solution(mesh):
    return jax.shard_map(
        body,
        mesh=mesh,
        in_specs=(
            P("dp", "col"),
            P("dp", "col"),
            P("dp"),
            P("col", "row", None, None, None),
            P("col", "row", None),
            P("col", "row", None),
            P("row", "col", None, None, None),
            P("row", "col", None),
            P("row", "col", None),
        ),
        out_specs=(
            P("dp", "col"),
            P("dp", "col"),
            P("col", "row", "dp", None, None),
            P("row", "col", "dp", None, None),
        ),
        check_vma=False,
    )
```

```python
import jax
import jax.numpy as jnp
from jax import lax
from jax.experimental import pallas as pl
from jax.experimental.pallas import tpu as pltpu
from jax.sharding import PartitionSpec as P

MESH = pl.DeviceIdType.MESH
BF = jnp.bfloat16
F32 = jnp.float32
B = 128
CAP = 256
MB_TOK = 64
COLS = 8
STEPS = 16
TD = 8
NB = 32
LATE, NEAR, FAR = 4, 14, 18
CH = B + 16
QR = 32
HW = 512

NT = (((1,), (1,)), ((), ()))
NN = (((1,), (0,)), ((), ()))


def dot(a, b, dims=NN):
    return lax.dot_general(a, b, dims, preferred_element_type=F32)


def kernel(
    counts, up_rows, up_cols, down_rows, down_cols,
    tokens_in, cotangent_in, up_in, down_in,
    y_out, g_out, gu_out, gd_out,
    tokens, cotangent, up_blocks, down_blocks, inv_v, inv_s, gm, tok_t, gm_t, wup, wdn, part, rbuf, ah, acts, yacc, gacc,
    fs, fr, ys, yr, yo, gbuf, xr, zbuf, zr,
    in_s, inv_sem, rs_s, rs_r, ag_s, ag_r, f_s, f_r, y_s, y_r, ya_s, ya_r, sb_s, sb_r, x_s, x_r, z_s, z_r,
):
    loads = [
        pltpu.make_async_copy(src, dst, in_s.at[i])
        for i, (src, dst) in enumerate(
            ((tokens_in, tokens), (up_in, up_blocks), (cotangent_in, cotangent), (down_in, down_blocks))
        )
    ]
    for load in loads:
        load.start()

    c = lax.axis_index("col")
    row = lax.axis_index("row")
    dp = lax.axis_index("dp")
    core = row % 2
    yi = row // 2
    hi = dp // 4
    xi = dp % 4
    count = counts[0]

    sibling = {"row": row + 1 - 2 * core}
    y_right = {"row": (row + 2) % 8}
    y_left = {"row": (row + 6) % 8}
    x_right = {"dp": hi * 4 + (xi + 1) % 4}
    x_left = {"dp": hi * 4 + (xi + 3) % 4}
    z_right = {"dp": ((hi + 1) % 4) * 4 + xi}
    z_left = {"dp": ((hi + 3) % 4) * 4 + xi}

    def send(src, dst, s_sem, r_sem, device):
        return pltpu.make_async_remote_copy(
            src_ref=src, dst_ref=dst, send_sem=s_sem, recv_sem=r_sem,
            device_id=device, device_id_type=MESH,
        )

    barrier = pltpu.get_barrier_semaphore()
    for peer in (sibling, y_right, y_left, x_right, x_left, z_right, z_left):
        pl.semaphore_signal(barrier, inc=1, device_id=peer, device_id_type=MESH)

    @pl.when(c > 0)
    def _():
        pl.semaphore_signal(barrier, inc=1, device_id={"col": c - 1}, device_id_type=MESH)

    @pl.when(c < 3)
    def _():
        pl.semaphore_signal(barrier, inc=1, device_id={"col": c + 1}, device_id_type=MESH)

    lane = lax.broadcasted_iota(jnp.int32, (8, B), 1)
    for tile, (rows_in, cols_in, wide) in enumerate(((up_rows, up_cols, 16), (down_rows, down_cols, TD))):
        table = jnp.full((8, B), NB, jnp.int32)
        for k in range(NB):
            table = jnp.where(lane == rows_in[k] * wide + cols_in[k], k, table)
        inv_v[tile] = table
    tables = pltpu.make_async_copy(inv_v, inv_s, inv_sem)
    tables.start()

    live = (lax.broadcasted_iota(jnp.int32, (CAP, 1), 0) // MB_TOK < count).astype(F32)
    loads[2].wait()
    gm[...] = (cotangent[...].astype(F32) * live).astype(BF)
    loads[0].wait()
    loads[1].wait()
    loads[3].wait()
    tables.wait()

    inside = jnp.where((c > 0) & (c < 3), 1, 0)
    pl.semaphore_wait(barrier, 8 + inside)

    def place(s):
        q = c + s * (3 - 2 * c)
        return q, c + 1 - 2 * s, c - 1 + 2 * s

    def rs_copy(u, s, device):
        ref = rbuf.at[s * COLS + u % COLS, u // COLS]
        j = s * STEPS + u
        return send(ref, ref, rs_s.at[j], rs_r.at[j], {"col": device})

    def ag_copy(u, s, device):
        ref = ah.at[s * COLS + u % COLS, u // COLS]
        j = s * STEPS + u
        return send(ref, ref, ag_s.at[j], ag_r.at[j], {"col": device})

    def enter(k, kind, both):
        for s in range(2):
            part[k + COLS * s, kind] = both[:, s * B:(s + 1) * B]

        @pl.when(c == 0)
        def _():
            rbuf[k, kind] = both[:, :B].astype(BF)
            rs_copy(k + COLS * kind, 0, 1).start()

        @pl.when(c == 3)
        def _():
            rbuf[k + COLS, kind] = both[:, B:].astype(BF)
            rs_copy(k + COLS * kind, 1, 2).start()

    def hidden_partials(k, carry):
        for s in range(2):
            for i in range(TD):
                iu = inv_s[0, 0, i * 16 + k + COLS * s]
                blk = up_blocks[jnp.minimum(iu, NB - 1)]
                wup[k, i * B:(i + 1) * B, s * B:(s + 1) * B] = jnp.where(iu < NB, blk, jnp.zeros_like(blk))
        enter(k, 0, dot(tokens[...], wup[k]))
        return carry

    def act_partials(k, carry):
        for s in range(2):
            for i in range(TD):
                idn = inv_s[1, 0, (k + COLS * s) * TD + i]
                blk = down_blocks[jnp.minimum(idn, NB - 1)]
                wdn[k, s * B:(s + 1) * B, i * B:(i + 1) * B] = jnp.where(idn < NB, blk, jnp.zeros_like(blk))
        enter(k, 1, dot(gm[...], wdn[k], NT))
        return carry

    lax.fori_loop(0, COLS, hidden_partials, 0)
    lax.fori_loop(0, COLS, act_partials, 0)

    yacc[...] = jnp.zeros_like(yacc)
    gacc[...] = jnp.zeros_like(gacc)
    for i in range(TD):
        tok_t[i] = tokens[:, i * B:(i + 1) * B].T
        gm_t[i] = gm[:, i * B:(i + 1) * B].T

    first = c // 2

    def sum_step(u, s):
        q, nxt, prv = place(s)
        j = s * COLS + u % COLS
        kind = u // COLS

        @pl.when(q > 0)
        def _():
            rs_copy(u, s, nxt).wait_recv()

        @pl.when((q > 0) & (q < 3))
        def _():
            rbuf[j, kind] = (rbuf[j, kind].astype(F32) + part[j, kind]).astype(BF)
            rs_copy(u, s, nxt).start()

        @pl.when((q == 3) & (kind == 0))
        def _():
            h = rbuf[j, 0].astype(F32) + part[j, 0]
            cdf = 0.5 * (1.0 + lax.erf(h * 0.7071067811865476))
            ah[j, 0] = (h * cdf).astype(BF)
            ag_copy(u, s, prv).start()
            part[j, 0] = cdf + h * jnp.exp(-0.5 * h * h) * 0.3989422804014327

        @pl.when((q == 3) & (kind == 1))
        def _():
            a = rbuf[j, 1].astype(F32) + part[j, 1]
            ah[j, 1] = (a * part[j, 0]).astype(BF)
            ag_copy(u, s, prv).start()

    def share_step(u, s):
        q, nxt, prv = place(s)

        @pl.when(q < 3)
        def _():
            ag_copy(u, s, prv).wait_recv()

        @pl.when((q > 0) & (q < 3))
        def _():
            ag_copy(u, s, prv).start()

    def line(kind):
        def body(it, carry):
            def during(lag, step):
                pl.when((it >= lag) & (it < lag + STEPS))(lambda: step(it - lag))

            if kind == 0:
                during(0, lambda u: sum_step(u, first))
                during(LATE, lambda u: sum_step(u, 1 - first))
            during(NEAR, lambda u: share_step(u, 1 - first))

            def last(u):
                share_step(u, first)
                k = u % COLS
                one, two = ah[k, kind], ah[k + COLS, kind]
                both = jnp.concatenate([one, two], axis=1)
                if kind == 0:
                    acts[k] = one
                    acts[k + COLS] = two
                    yacc[...] += dot(both, wdn[k])
                else:
                    gacc[...] += dot(both, wup[k], NT)

            during(FAR, last)
            return carry

        return body

    count_rows = jnp.zeros((16, B), F32) + count.astype(F32)

    order = [(hi + 2) % 4, (hi + 1) % 4, (hi + 3) % 4, hi]
    x1, x2, x3 = (xi + 1) % 4, (xi + 2) % 4, (xi + 3) % 4
    y1, y2, y3 = (yi + 1) % 4, (yi + 2) % 4, (yi + 3) % 4

    def size(arr, b):
        return CH if arr == 1 and b == 0 else B

    def grads(arr, g):
        def body(xq, carry):
            for b in range(2):
                k = (order[g] * 4 + xq) * 2 + b
                if arr == 0:
                    block = dot(gm_t[down_cols[k]], acts[down_rows[k]])
                else:
                    block = dot(tok_t[up_rows[k]], ah[up_cols[k], 1])
                gbuf[arr, g, xq, b, :B, :] = block.astype(BF)
            if arr == 1:
                gbuf[arr, g, xq, 0, B:, :] = count_rows.astype(BF)
            return carry

        lax.fori_loop(0, 4, body, 0)

    def half_of(m):
        return (0, 1, 1, 0, 0, 1)[m]

    def x_msg(arr, g, m):
        b = half_of(m)
        rows = pl.ds(0, size(arr, b))
        place_of = (x2, x2, x1, x3)
        src = gbuf.at[arr, g, place_of[m], b, rows] if m < 4 else xr.at[arr, g, m - 4, rows]
        return send(
            src, xr.at[arr, g, m, rows], x_s.at[arr, g, m], x_r.at[arr, g, m], x_left if m % 2 else x_right
        )

    def x_start(arr, g):
        for m in range(4):
            x_msg(arr, g, m).start()

    def x_relay(arr, g):
        for m in range(2):
            n = size(arr, m)
            x_msg(arr, g, m).wait_recv()
            near = x3 if m else x1
            xr[arr, g, m, :n] = (xr[arr, g, m, :n].astype(F32) + gbuf[arr, g, near, m, :n].astype(F32)).astype(BF)
            x_msg(arr, g, m + 4).start()

    def x_final(arr, g):
        for m in range(2, 6):
            x_msg(arr, g, m).wait_recv()
        for b in range(2):
            n = size(arr, b)
            one, two = (2, 5) if b else (3, 4)
            full = gbuf[arr, g, xi, b, :n].astype(F32) + xr[arr, g, one, :n].astype(F32)
            zbuf[arr, g, b, :n] = (full + xr[arr, g, two, :n].astype(F32)).astype(BF)

    def z_msg(arr, m):
        b = half_of(m)
        rows = pl.ds(0, size(arr, b))
        src = zbuf.at[arr, (0, 0, 1, 2)[m], b, rows] if m < 4 else zr.at[arr, m - 4, rows]
        return send(src, zr.at[arr, m, rows], z_s.at[arr, m], z_r.at[arr, m], z_left if m % 2 else z_right)

    def z_relay(arr, m):
        n = size(arr, m)
        z_msg(arr, m).wait_recv()
        zr[arr, m, :n] = (zr[arr, m, :n].astype(F32) + zbuf[arr, 1 + m, m, :n].astype(F32)).astype(BF)
        z_msg(arr, m + 4).start()

    def z_final(arr, b):
        for m in (2, 5) if b else (3, 4):
            z_msg(arr, m).wait_recv()
        n = size(arr, b)
        one, two = (2, 5) if b else (3, 4)
        return zbuf[arr, 3, b, :n].astype(F32) + zr[arr, one, :n].astype(F32) + zr[arr, two, :n].astype(F32)

    accs = (yacc, gacc)
    mine = pl.multiple_of(core * B, B)
    other = pl.multiple_of((1 - core) * B, B)

    def pair(a):
        return send(fs.at[a], fr.at[a], f_s.at[a], f_r.at[a], sibling)

    def term(a, chunk, half):
        rows = pl.ds(pl.multiple_of(core * B + chunk * QR, QR), QR)
        return accs[a][rows, half * HW:(half + 1) * HW]

    def row_msg(a, m):
        src = ys.at[a, m] if m < 4 else yr.at[a, m - 4]
        return send(src, yr.at[a, m], y_s.at[a, m], y_r.at[a, m], y_left if m % 2 else y_right)

    def share_ref(a, chunk, m):
        return yo.at[core * 4 + chunk, a, half_of(m) if m in (2, 3) else m % 2]

    def share_msg(a, m):
        ref = share_ref(a, (yi, yi, yi, yi, y3, y1)[m], m)
        return send(ref, ref, ya_s.at[a, m], ya_r.at[a, m], y_left if m % 2 else y_right)

    def share_in(a, m):
        ref = share_ref(a, (y3, y1, y3, y1, y2, y2)[m], m)
        return send(ref, ref, ya_s.at[a, m], ya_r.at[a, m], y_left if m % 2 else y_right)

    def twin(a, m, half):
        ref = yo.at[half * 4 + (yi, y3, y1, y2)[m], a]
        return send(ref, ref, sb_s.at[a, m], sb_r.at[a, m], sibling)

    def row_pair(a):
        fs[a] = accs[a][pl.ds(other, B), :].astype(BF)
        pair(a).start()

    def row_start(a):
        pair(a).wait_recv()
        accs[a][pl.ds(mine, B), :] += fr[a].astype(F32)
        for m in range(4):
            ys[a, m] = term(a, (y2, y2, y1, y3)[m], half_of(m)).astype(BF)
            row_msg(a, m).start()

    def row_relay(a):
        for m in range(2):
            row_msg(a, m).wait_recv()
            yr[a, m] = (yr[a, m].astype(F32) + term(a, (y1, y3)[m], m)).astype(BF)
            row_msg(a, m + 4).start()

    def row_final(a):
        for m in range(2, 6):
            row_msg(a, m).wait_recv()
        for b in range(2):
            one, two = (2, 5) if b else (3, 4)
            full = term(a, yi, b) + yr[a, one].astype(F32) + yr[a, two].astype(F32)
            if a == 0:
                full = full * (core * 2 + yi // 2 < count).astype(F32)
            yo[core * 4 + yi, a, b] = full.astype(BF)
        for m in range(4):
            share_msg(a, m).start()
        twin(a, 0, core).start()

    def row_pass(a):
        for m in range(2):
            share_in(a, m).wait_recv()
            share_msg(a, m + 4).start()
        for m in range(2):
            share_in(a, m + 2).wait_recv()
            twin(a, m + 1, core).start()

    def row_end(a):
        share_in(a, 4).wait_recv()
        share_in(a, 5).wait_recv()
        twin(a, 3, core).start()

    def row_out(a, out):
        for m in range(4):
            twin(a, m, 1 - core).wait_recv()
        for chunk in range(8):
            for b in range(2):
                out[chunk * QR:(chunk + 1) * QR, b * HW:(b + 1) * HW] = yo[chunk, a, b]

    after = FAR + COLS
    lax.fori_loop(0, after, line(0), 0)

    def on(first_step, steps):
        lax.fori_loop(after + first_step, after + first_step + steps, line(1), 0)

    row_pair(0)
    grads(0, 0)
    x_start(0, 0)
    grads(0, 1)
    x_start(0, 1)
    on(0, 1)
    grads(0, 2)
    x_start(0, 2)
    grads(0, 3)
    x_start(0, 3)
    on(1, 1)
    row_start(0)
    x_relay(0, 0)
    on(2, 2)
    x_relay(0, 1)
    row_relay(0)
    on(4, 1)
    x_relay(0, 2)
    x_relay(0, 3)
    on(5, 1)
    row_final(0)
    x_final(0, 0)
    z_msg(0, 0).start()
    z_msg(0, 1).start()
    on(6, 2)

    row_pair(1)
    grads(1, 0)
    x_start(1, 0)
    x_final(0, 1)
    z_msg(0, 2).start()
    x_final(0, 2)
    z_msg(0, 3).start()
    grads(1, 1)
    x_start(1, 1)
    row_start(1)
    x_relay(1, 0)
    grads(1, 2)
    x_start(1, 2)
    z_relay(0, 0)
    z_relay(0, 1)
    x_relay(1, 1)
    row_relay(1)
    grads(1, 3)
    x_start(1, 3)
    x_final(1, 0)
    z_msg(1, 0).start()
    z_msg(1, 1).start()
    x_relay(1, 2)
    row_pass(0)
    row_final(1)
    x_final(1, 1)
    z_msg(1, 2).start()
    x_relay(1, 3)
    x_final(1, 2)
    z_msg(1, 3).start()
    row_end(0)
    row_pass(1)
    x_final(0, 3)
    x_final(1, 3)
    row_out(0, y_out)
    down0 = z_final(0, 0)
    down1 = z_final(0, 1)
    row_end(1)
    z_relay(1, 0)
    z_relay(1, 1)
    row_out(1, g_out)

    up0 = z_final(1, 0)
    total = up0[B:B + 1, :]
    gu_out[0] = up0[:B, :] / total
    gd_out[0] = (down0 / total).T
    gd_out[1] = (down1 / total).T
    gu_out[1] = z_final(1, 1) / total

    for s in range(2):
        q, nxt, prv = place(s)

        @pl.when(q < 3)
        def _(s=s, nxt=nxt):
            lax.fori_loop(0, STEPS, lambda u, v: (rs_copy(u, s, nxt).wait_send(), v)[1], 0)

        @pl.when(q > 0)
        def _(s=s, prv=prv):
            lax.fori_loop(0, STEPS, lambda u, v: (ag_copy(u, s, prv).wait_send(), v)[1], 0)

    for arr in range(2):
        pair(arr).wait_send()
        for m in range(6):
            row_msg(arr, m).wait_send()
            share_msg(arr, m).wait_send()
            z_msg(arr, m).wait_send()
            for g in range(4):
                x_msg(arr, g, m).wait_send()
        for m in range(4):
            twin(arr, m, core).wait_send()


def store(y, g, u, d, y_to, g_to, u_to, d_to, y_v, g_v, u_v, d_v, in_sem, out_sem):
    arrays = ((y, y_v, y_to), (g, g_v, g_to), (u, u_v, u_to), (d, d_v, d_to))
    into = [pltpu.make_async_copy(src, mid, in_sem.at[i]) for i, (src, mid, dst) in enumerate(arrays)]
    out = [pltpu.make_async_copy(mid, dst, out_sem.at[i]) for i, (src, mid, dst) in enumerate(arrays)]
    for copy in into:
        copy.start()
    for i in range(4):
        into[i].wait()
        out[i].start()
    for copy in out:
        copy.wait()


def body(tokens, cotangent, counts, up_blocks, up_rows, up_cols, down_blocks, down_rows, down_cols):
    ur, uc = up_rows[0, 0], up_cols[0, 0]
    dr, dc = down_rows[0, 0], down_cols[0, 0]
    smem = pl.BlockSpec(memory_space=pltpu.SMEM)
    vmem = pl.BlockSpec(memory_space=pltpu.VMEM)
    hbm = pl.BlockSpec(memory_space=pltpu.HBM)
    width = TD * B
    dma = pltpu.SemaphoreType.DMA
    shapes = (
        jax.ShapeDtypeStruct((CAP, width), BF),
        jax.ShapeDtypeStruct((CAP, width), BF),
        jax.ShapeDtypeStruct((2, B, B), F32),
        jax.ShapeDtypeStruct((2, B, B), F32),
    )
    results = pl.pallas_call(
        kernel,
        out_shape=shapes,
        in_specs=[smem] * 5 + [hbm] * 4,
        out_specs=(vmem,) * 4,
        scratch_shapes=[
            pltpu.VMEM((CAP, width), BF),
            pltpu.VMEM((CAP, width), BF),
            pltpu.VMEM((NB, B, B), BF),
            pltpu.VMEM((NB, B, B), BF),
            pltpu.VMEM((2, 8, B), jnp.int32),
            pltpu.SMEM((2, 8, B), jnp.int32),
            pltpu.VMEM((CAP, width), BF),
            pltpu.VMEM((TD, B, CAP), BF),
            pltpu.VMEM((TD, B, CAP), BF),
            pltpu.VMEM((STEPS, width, 2 * B), BF),
            pltpu.VMEM((STEPS, 2 * B, width), BF),
            pltpu.VMEM((16, 2, CAP, B), F32),
            pltpu.VMEM((16, 2, CAP, B), BF),
            pltpu.VMEM((16, 2, CAP, B), BF),
            pltpu.VMEM((16, CAP, B), BF),
            pltpu.VMEM((CAP, width), F32),
            pltpu.VMEM((CAP, width), F32),
            pltpu.VMEM((2, B, width), BF),
            pltpu.VMEM((2, B, width), BF),
            pltpu.VMEM((2, 4, QR, HW), BF),
            pltpu.VMEM((2, 6, QR, HW), BF),
            pltpu.VMEM((8, 2, 2, QR, HW), BF),
            pltpu.VMEM((2, 4, 4, 2, CH, B), BF),
            pltpu.VMEM((2, 4, 6, CH, B), BF),
            pltpu.VMEM((2, 4, 2, CH, B), BF),
            pltpu.VMEM((2, 6, CH, B), BF),
            dma((4,)), dma, dma((32,)), dma((32,)), dma((32,)), dma((32,)),
            dma((2,)), dma((2,)), dma((2, 6)), dma((2, 6)), dma((2, 6)), dma((2, 6)), dma((2, 4)), dma((2, 4)),
            dma((2, 4, 6)), dma((2, 4, 6)), dma((2, 6)), dma((2, 6)),
        ],
        compiler_params=pltpu.CompilerParams(
            collective_id=0, has_side_effects=True, vmem_limit_bytes=56 << 20
        ),
    )(counts, ur, uc, dr, dc, tokens, cotangent, up_blocks[0, 0], down_blocks[0, 0])
    y_out, g_out, gu, gd = pl.pallas_call(
        store,
        out_shape=shapes,
        in_specs=[hbm] * 4,
        out_specs=(hbm,) * 4,
        scratch_shapes=[pltpu.VMEM(shape.shape, shape.dtype) for shape in shapes] + [dma((4,)), dma((4,))],
    )(*results)
    return y_out, g_out, gu[None, None], gd[None, None]


def solution(mesh):
    return jax.shard_map(
        body,
        mesh=mesh,
        in_specs=(
            P("dp", "col"),
            P("dp", "col"),
            P("dp"),
            P("col", "row", None, None, None),
            P("col", "row", None),
            P("col", "row", None),
            P("row", "col", None, None, None),
            P("row", "col", None),
            P("row", "col", None),
        ),
        out_specs=(
            P("dp", "col"),
            P("dp", "col"),
            P("col", "row", "dp", None, None),
            P("row", "col", "dp", None, None),
        ),
        check_vma=False,
    )
```

```python
import jax
import jax.numpy as jnp
from jax import lax
from jax.experimental import pallas as pl
from jax.experimental.pallas import tpu as pltpu
from jax.sharding import PartitionSpec as P

MESH = pl.DeviceIdType.MESH
BF = jnp.bfloat16
F32 = jnp.float32
B = 128
CAP = 256
MB_TOK = 64
COLS = 8
STEPS = 16
TD = 8
NB = 32
LATE, NEAR, FAR = 4, 14, 18
CH = B + 16
QR = 32
HW = 512

NT = (((1,), (1,)), ((), ()))
NN = (((1,), (0,)), ((), ()))


def dot(a, b, dims=NN):
    return lax.dot_general(a, b, dims, preferred_element_type=F32)


def kernel(
    counts, up_rows, up_cols, down_rows, down_cols,
    tokens_in, cotangent_in, up_in, down_in,
    y_out, g_out, gu_out, gd_out,
    tokens, cotangent, up_blocks, down_blocks, inv_v, inv_s, gm, tok_t, gm_t, wup, wdn, part, rbuf, ah, acts, yacc, gacc,
    fs, fr, ys, yr, yo, gbuf, xr, zbuf, zr,
    in_s, inv_sem, rs_s, rs_r, ag_s, ag_r, f_s, f_r, y_s, y_r, ya_s, ya_r, sb_s, sb_r, x_s, x_r, z_s, z_r,
):
    loads = [
        pltpu.make_async_copy(src, dst, in_s.at[i])
        for i, (src, dst) in enumerate(
            ((tokens_in, tokens), (up_in, up_blocks), (cotangent_in, cotangent), (down_in, down_blocks))
        )
    ]
    for load in loads:
        load.start()

    c = lax.axis_index("col")
    row = lax.axis_index("row")
    dp = lax.axis_index("dp")
    core = row % 2
    yi = row // 2
    hi = dp // 4
    xi = dp % 4
    count = counts[0]

    sibling = {"row": row + 1 - 2 * core}
    y_right = {"row": (row + 2) % 8}
    y_left = {"row": (row + 6) % 8}
    x_right = {"dp": hi * 4 + (xi + 1) % 4}
    x_left = {"dp": hi * 4 + (xi + 3) % 4}
    z_right = {"dp": ((hi + 1) % 4) * 4 + xi}
    z_left = {"dp": ((hi + 3) % 4) * 4 + xi}

    def send(src, dst, s_sem, r_sem, device):
        return pltpu.make_async_remote_copy(
            src_ref=src, dst_ref=dst, send_sem=s_sem, recv_sem=r_sem,
            device_id=device, device_id_type=MESH,
        )

    barrier = pltpu.get_barrier_semaphore()
    for peer in (sibling, y_right, y_left, x_right, x_left, z_right, z_left):
        pl.semaphore_signal(barrier, inc=1, device_id=peer, device_id_type=MESH)

    @pl.when(c > 0)
    def _():
        pl.semaphore_signal(barrier, inc=1, device_id={"col": c - 1}, device_id_type=MESH)

    @pl.when(c < 3)
    def _():
        pl.semaphore_signal(barrier, inc=1, device_id={"col": c + 1}, device_id_type=MESH)

    lane = lax.broadcasted_iota(jnp.int32, (8, B), 1)
    for tile, (rows_in, cols_in, wide) in enumerate(((up_rows, up_cols, 16), (down_rows, down_cols, TD))):
        table = jnp.full((8, B), NB, jnp.int32)
        for k in range(NB):
            table = jnp.where(lane == rows_in[k] * wide + cols_in[k], k, table)
        inv_v[tile] = table
    tables = pltpu.make_async_copy(inv_v, inv_s, inv_sem)
    tables.start()

    live = (lax.broadcasted_iota(jnp.int32, (CAP, 1), 0) // MB_TOK < count).astype(F32)
    loads[2].wait()
    gm[...] = (cotangent[...].astype(F32) * live).astype(BF)
    loads[0].wait()
    loads[1].wait()
    loads[3].wait()
    tables.wait()

    inside = jnp.where((c > 0) & (c < 3), 1, 0)
    pl.semaphore_wait(barrier, 8 + inside)

    def place(s):
        q = c + s * (3 - 2 * c)
        return q, c + 1 - 2 * s, c - 1 + 2 * s

    def rs_copy(u, s, device):
        ref = rbuf.at[s * COLS + u % COLS, u // COLS]
        j = s * STEPS + u
        return send(ref, ref, rs_s.at[j], rs_r.at[j], {"col": device})

    def ag_copy(u, s, device):
        ref = ah.at[s * COLS + u % COLS, u // COLS]
        j = s * STEPS + u
        return send(ref, ref, ag_s.at[j], ag_r.at[j], {"col": device})

    def enter(k, kind, both):
        for s in range(2):
            part[k + COLS * s, kind] = both[:, s * B:(s + 1) * B]

        @pl.when(c == 0)
        def _():
            rbuf[k, kind] = both[:, :B].astype(BF)
            rs_copy(k + COLS * kind, 0, 1).start()

        @pl.when(c == 3)
        def _():
            rbuf[k + COLS, kind] = both[:, B:].astype(BF)
            rs_copy(k + COLS * kind, 1, 2).start()

    def hidden_partials(k, carry):
        for s in range(2):
            for i in range(TD):
                iu = inv_s[0, 0, i * 16 + k + COLS * s]
                blk = up_blocks[jnp.minimum(iu, NB - 1)]
                wup[k, i * B:(i + 1) * B, s * B:(s + 1) * B] = jnp.where(iu < NB, blk, jnp.zeros_like(blk))
        enter(k, 0, dot(tokens[...], wup[k]))
        return carry

    def act_partials(k, carry):
        for s in range(2):
            for i in range(TD):
                idn = inv_s[1, 0, (k + COLS * s) * TD + i]
                blk = down_blocks[jnp.minimum(idn, NB - 1)]
                wdn[k, s * B:(s + 1) * B, i * B:(i + 1) * B] = jnp.where(idn < NB, blk, jnp.zeros_like(blk))
        enter(k, 1, dot(gm[...], wdn[k], NT))
        return carry

    lax.fori_loop(0, COLS, hidden_partials, 0)
    lax.fori_loop(0, COLS, act_partials, 0)

    yacc[...] = jnp.zeros_like(yacc)
    gacc[...] = jnp.zeros_like(gacc)
    def transposes(i):
        columns = pl.ds(pl.multiple_of(i * B, B), B)
        tok_t[i] = tokens[:, columns].T
        gm_t[i] = gm[:, columns].T

    first = c // 2

    def sum_step(u, s):
        q, nxt, prv = place(s)
        j = s * COLS + u % COLS
        kind = u // COLS

        @pl.when(q > 0)
        def _():
            rs_copy(u, s, nxt).wait_recv()

        @pl.when((q > 0) & (q < 3))
        def _():
            rbuf[j, kind] = (rbuf[j, kind].astype(F32) + part[j, kind]).astype(BF)
            rs_copy(u, s, nxt).start()

        @pl.when((q == 3) & (kind == 0))
        def _():
            h = rbuf[j, 0].astype(F32) + part[j, 0]
            cdf = 0.5 * (1.0 + lax.erf(h * 0.7071067811865476))
            ah[j, 0] = (h * cdf).astype(BF)
            ag_copy(u, s, prv).start()
            part[j, 0] = cdf + h * jnp.exp(-0.5 * h * h) * 0.3989422804014327

        @pl.when((q == 3) & (kind == 1))
        def _():
            a = rbuf[j, 1].astype(F32) + part[j, 1]
            ah[j, 1] = (a * part[j, 0]).astype(BF)
            ag_copy(u, s, prv).start()

    def share_step(u, s):
        q, nxt, prv = place(s)

        @pl.when(q < 3)
        def _():
            ag_copy(u, s, prv).wait_recv()

        @pl.when((q > 0) & (q < 3))
        def _():
            ag_copy(u, s, prv).start()

    def line(kind):
        def body(it, carry):
            def during(lag, step):
                pl.when((it >= lag) & (it < lag + STEPS))(lambda: step(it - lag))

            if kind == 0:
                during(0, lambda u: sum_step(u, first))
                during(LATE, lambda u: sum_step(u, 1 - first))
                pl.when((it >= COLS) & (it < 2 * COLS))(lambda: transposes(it - COLS))
            during(NEAR, lambda u: share_step(u, 1 - first))

            def last(u):
                share_step(u, first)
                k = u % COLS
                one, two = ah[k, kind], ah[k + COLS, kind]
                both = jnp.concatenate([one, two], axis=1)
                if kind == 0:
                    acts[k] = one
                    acts[k + COLS] = two
                    yacc[...] += dot(both, wdn[k])
                else:
                    gacc[...] += dot(both, wup[k], NT)

            during(FAR, last)
            return carry

        return body

    count_rows = jnp.zeros((16, B), F32) + count.astype(F32)

    order = [(hi + 2) % 4, (hi + 1) % 4, (hi + 3) % 4, hi]
    x1, x2, x3 = (xi + 1) % 4, (xi + 2) % 4, (xi + 3) % 4
    y1, y2, y3 = (yi + 1) % 4, (yi + 2) % 4, (yi + 3) % 4

    def size(arr, b):
        return CH if arr == 1 and b == 0 else B

    def grads(arr, g):
        def body(xq, carry):
            for b in range(2):
                k = (order[g] * 4 + xq) * 2 + b
                if arr == 0:
                    block = dot(gm_t[down_cols[k]], acts[down_rows[k]])
                else:
                    block = dot(tok_t[up_rows[k]], ah[up_cols[k], 1])
                gbuf[arr, g, xq, b, :B, :] = block.astype(BF)
            if arr == 1:
                gbuf[arr, g, xq, 0, B:, :] = count_rows.astype(BF)
            return carry

        lax.fori_loop(0, 4, body, 0)

    def half_of(m):
        return (0, 1, 1, 0, 0, 1)[m]

    def x_msg(arr, g, m):
        b = half_of(m)
        rows = pl.ds(0, size(arr, b))
        place_of = (x2, x2, x1, x3)
        src = gbuf.at[arr, g, place_of[m], b, rows] if m < 4 else xr.at[arr, g, m - 4, rows]
        return send(
            src, xr.at[arr, g, m, rows], x_s.at[arr, g, m], x_r.at[arr, g, m], x_left if m % 2 else x_right
        )

    def x_start(arr, g):
        for m in range(4):
            x_msg(arr, g, m).start()

    def x_relay(arr, g):
        for m in range(2):
            n = size(arr, m)
            x_msg(arr, g, m).wait_recv()
            near = x3 if m else x1
            xr[arr, g, m, :n] = (xr[arr, g, m, :n].astype(F32) + gbuf[arr, g, near, m, :n].astype(F32)).astype(BF)
            x_msg(arr, g, m + 4).start()

    def x_final(arr, g):
        for m in range(2, 6):
            x_msg(arr, g, m).wait_recv()
        for b in range(2):
            n = size(arr, b)
            one, two = (2, 5) if b else (3, 4)
            full = gbuf[arr, g, xi, b, :n].astype(F32) + xr[arr, g, one, :n].astype(F32)
            zbuf[arr, g, b, :n] = (full + xr[arr, g, two, :n].astype(F32)).astype(BF)

    def z_msg(arr, m):
        b = half_of(m)
        rows = pl.ds(0, size(arr, b))
        src = zbuf.at[arr, (0, 0, 1, 2)[m], b, rows] if m < 4 else zr.at[arr, m - 4, rows]
        return send(src, zr.at[arr, m, rows], z_s.at[arr, m], z_r.at[arr, m], z_left if m % 2 else z_right)

    def z_relay(arr, m):
        n = size(arr, m)
        z_msg(arr, m).wait_recv()
        zr[arr, m, :n] = (zr[arr, m, :n].astype(F32) + zbuf[arr, 1 + m, m, :n].astype(F32)).astype(BF)
        z_msg(arr, m + 4).start()

    def z_final(arr, b):
        for m in (2, 5) if b else (3, 4):
            z_msg(arr, m).wait_recv()
        n = size(arr, b)
        one, two = (2, 5) if b else (3, 4)
        return zbuf[arr, 3, b, :n].astype(F32) + zr[arr, one, :n].astype(F32) + zr[arr, two, :n].astype(F32)

    accs = (yacc, gacc)
    mine = pl.multiple_of(core * B, B)
    other = pl.multiple_of((1 - core) * B, B)

    def pair(a):
        return send(fs.at[a], fr.at[a], f_s.at[a], f_r.at[a], sibling)

    def term(a, chunk, half):
        rows = pl.ds(pl.multiple_of(core * B + chunk * QR, QR), QR)
        return accs[a][rows, half * HW:(half + 1) * HW]

    def row_msg(a, m):
        src = ys.at[a, m] if m < 4 else yr.at[a, m - 4]
        return send(src, yr.at[a, m], y_s.at[a, m], y_r.at[a, m], y_left if m % 2 else y_right)

    def share_ref(a, chunk, m):
        return yo.at[core * 4 + chunk, a, half_of(m) if m in (2, 3) else m % 2]

    def share_msg(a, m):
        ref = share_ref(a, (yi, yi, yi, yi, y3, y1)[m], m)
        return send(ref, ref, ya_s.at[a, m], ya_r.at[a, m], y_left if m % 2 else y_right)

    def share_in(a, m):
        ref = share_ref(a, (y3, y1, y3, y1, y2, y2)[m], m)
        return send(ref, ref, ya_s.at[a, m], ya_r.at[a, m], y_left if m % 2 else y_right)

    def twin(a, m, half):
        ref = yo.at[half * 4 + (yi, y3, y1, y2)[m], a]
        return send(ref, ref, sb_s.at[a, m], sb_r.at[a, m], sibling)

    def row_pair(a):
        fs[a] = accs[a][pl.ds(other, B), :].astype(BF)
        pair(a).start()

    def row_start(a):
        pair(a).wait_recv()
        accs[a][pl.ds(mine, B), :] += fr[a].astype(F32)
        for m in range(4):
            ys[a, m] = term(a, (y2, y2, y1, y3)[m], half_of(m)).astype(BF)
            row_msg(a, m).start()

    def row_relay(a):
        for m in range(2):
            row_msg(a, m).wait_recv()
            yr[a, m] = (yr[a, m].astype(F32) + term(a, (y1, y3)[m], m)).astype(BF)
            row_msg(a, m + 4).start()

    def row_final(a):
        for m in range(2, 6):
            row_msg(a, m).wait_recv()
        for b in range(2):
            one, two = (2, 5) if b else (3, 4)
            full = term(a, yi, b) + yr[a, one].astype(F32) + yr[a, two].astype(F32)
            if a == 0:
                full = full * (core * 2 + yi // 2 < count).astype(F32)
            yo[core * 4 + yi, a, b] = full.astype(BF)
        for m in range(4):
            share_msg(a, m).start()
        twin(a, 0, core).start()

    def row_pass(a):
        for m in range(2):
            share_in(a, m).wait_recv()
            share_msg(a, m + 4).start()
        for m in range(2):
            share_in(a, m + 2).wait_recv()
            twin(a, m + 1, core).start()

    def row_end(a):
        share_in(a, 4).wait_recv()
        share_in(a, 5).wait_recv()
        twin(a, 3, core).start()

    def row_out(a, out):
        for m in range(4):
            twin(a, m, 1 - core).wait_recv()
        for chunk in range(8):
            for b in range(2):
                out[chunk * QR:(chunk + 1) * QR, b * HW:(b + 1) * HW] = yo[chunk, a, b]

    after = FAR + COLS
    lax.fori_loop(0, after, line(0), 0)

    def on(first_step, steps):
        lax.fori_loop(after + first_step, after + first_step + steps, line(1), 0)

    row_pair(0)
    grads(0, 0)
    x_start(0, 0)
    grads(0, 1)
    x_start(0, 1)
    on(0, 1)
    grads(0, 2)
    x_start(0, 2)
    grads(0, 3)
    x_start(0, 3)
    on(1, 1)
    row_start(0)
    x_relay(0, 0)
    on(2, 2)
    x_relay(0, 1)
    row_relay(0)
    on(4, 1)
    x_relay(0, 2)
    x_relay(0, 3)
    on(5, 1)
    row_final(0)
    on(6, 2)

    row_pair(1)
    grads(1, 0)
    x_start(1, 0)
    x_final(0, 0)
    z_msg(0, 0).start()
    z_msg(0, 1).start()
    x_final(0, 1)
    z_msg(0, 2).start()
    x_final(0, 2)
    z_msg(0, 3).start()
    grads(1, 1)
    x_start(1, 1)
    row_start(1)
    x_relay(1, 0)
    grads(1, 2)
    x_start(1, 2)
    z_relay(0, 0)
    z_relay(0, 1)
    x_relay(1, 1)
    row_relay(1)
    grads(1, 3)
    x_start(1, 3)
    x_final(1, 0)
    z_msg(1, 0).start()
    z_msg(1, 1).start()
    x_relay(1, 2)
    row_pass(0)
    row_final(1)
    x_final(1, 1)
    z_msg(1, 2).start()
    x_relay(1, 3)
    x_final(1, 2)
    z_msg(1, 3).start()
    row_end(0)
    row_pass(1)
    x_final(0, 3)
    x_final(1, 3)
    row_out(0, y_out)
    down0 = z_final(0, 0)
    down1 = z_final(0, 1)
    z_relay(1, 0)
    z_relay(1, 1)
    row_end(1)
    row_out(1, g_out)

    up0 = z_final(1, 0)
    total = up0[B:B + 1, :]
    gu_out[0] = up0[:B, :] / total
    gd_out[0] = (down0 / total).T
    gd_out[1] = (down1 / total).T
    gu_out[1] = z_final(1, 1) / total

    for s in range(2):
        q, nxt, prv = place(s)

        @pl.when(q < 3)
        def _(s=s, nxt=nxt):
            lax.fori_loop(0, STEPS, lambda u, v: (rs_copy(u, s, nxt).wait_send(), v)[1], 0)

        @pl.when(q > 0)
        def _(s=s, prv=prv):
            lax.fori_loop(0, STEPS, lambda u, v: (ag_copy(u, s, prv).wait_send(), v)[1], 0)

    for arr in range(2):
        pair(arr).wait_send()
        for m in range(6):
            row_msg(arr, m).wait_send()
            share_msg(arr, m).wait_send()
            z_msg(arr, m).wait_send()
            for g in range(4):
                x_msg(arr, g, m).wait_send()
        for m in range(4):
            twin(arr, m, core).wait_send()


def store(y, g, u, d, y_to, g_to, u_to, d_to, y_v, g_v, u_v, d_v, in_sem, out_sem):
    arrays = ((y, y_v, y_to), (g, g_v, g_to), (u, u_v, u_to), (d, d_v, d_to))
    into = [pltpu.make_async_copy(src, mid, in_sem.at[i]) for i, (src, mid, dst) in enumerate(arrays)]
    out = [pltpu.make_async_copy(mid, dst, out_sem.at[i]) for i, (src, mid, dst) in enumerate(arrays)]
    for copy in into:
        copy.start()
    for i in range(4):
        into[i].wait()
        out[i].start()
    for copy in out:
        copy.wait()


def body(tokens, cotangent, counts, up_blocks, up_rows, up_cols, down_blocks, down_rows, down_cols):
    ur, uc = up_rows[0, 0], up_cols[0, 0]
    dr, dc = down_rows[0, 0], down_cols[0, 0]
    smem = pl.BlockSpec(memory_space=pltpu.SMEM)
    vmem = pl.BlockSpec(memory_space=pltpu.VMEM)
    hbm = pl.BlockSpec(memory_space=pltpu.HBM)
    width = TD * B
    dma = pltpu.SemaphoreType.DMA
    shapes = (
        jax.ShapeDtypeStruct((CAP, width), BF),
        jax.ShapeDtypeStruct((CAP, width), BF),
        jax.ShapeDtypeStruct((2, B, B), F32),
        jax.ShapeDtypeStruct((2, B, B), F32),
    )
    results = pl.pallas_call(
        kernel,
        out_shape=shapes,
        in_specs=[smem] * 5 + [hbm] * 4,
        out_specs=(vmem,) * 4,
        scratch_shapes=[
            pltpu.VMEM((CAP, width), BF),
            pltpu.VMEM((CAP, width), BF),
            pltpu.VMEM((NB, B, B), BF),
            pltpu.VMEM((NB, B, B), BF),
            pltpu.VMEM((2, 8, B), jnp.int32),
            pltpu.SMEM((2, 8, B), jnp.int32),
            pltpu.VMEM((CAP, width), BF),
            pltpu.VMEM((TD, B, CAP), BF),
            pltpu.VMEM((TD, B, CAP), BF),
            pltpu.VMEM((STEPS, width, 2 * B), BF),
            pltpu.VMEM((STEPS, 2 * B, width), BF),
            pltpu.VMEM((16, 2, CAP, B), F32),
            pltpu.VMEM((16, 2, CAP, B), BF),
            pltpu.VMEM((16, 2, CAP, B), BF),
            pltpu.VMEM((16, CAP, B), BF),
            pltpu.VMEM((CAP, width), F32),
            pltpu.VMEM((CAP, width), F32),
            pltpu.VMEM((2, B, width), BF),
            pltpu.VMEM((2, B, width), BF),
            pltpu.VMEM((2, 4, QR, HW), BF),
            pltpu.VMEM((2, 6, QR, HW), BF),
            pltpu.VMEM((8, 2, 2, QR, HW), BF),
            pltpu.VMEM((2, 4, 4, 2, CH, B), BF),
            pltpu.VMEM((2, 4, 6, CH, B), BF),
            pltpu.VMEM((2, 4, 2, CH, B), BF),
            pltpu.VMEM((2, 6, CH, B), BF),
            dma((4,)), dma, dma((32,)), dma((32,)), dma((32,)), dma((32,)),
            dma((2,)), dma((2,)), dma((2, 6)), dma((2, 6)), dma((2, 6)), dma((2, 6)), dma((2, 4)), dma((2, 4)),
            dma((2, 4, 6)), dma((2, 4, 6)), dma((2, 6)), dma((2, 6)),
        ],
        compiler_params=pltpu.CompilerParams(
            collective_id=0, has_side_effects=True, vmem_limit_bytes=56 << 20
        ),
    )(counts, ur, uc, dr, dc, tokens, cotangent, up_blocks[0, 0], down_blocks[0, 0])
    y_out, g_out, gu, gd = pl.pallas_call(
        store,
        out_shape=shapes,
        in_specs=[hbm] * 4,
        out_specs=(hbm,) * 4,
        scratch_shapes=[pltpu.VMEM(shape.shape, shape.dtype) for shape in shapes] + [dma((4,)), dma((4,))],
    )(*results)
    return y_out, g_out, gu[None, None], gd[None, None]


def solution(mesh):
    return jax.shard_map(
        body,
        mesh=mesh,
        in_specs=(
            P("dp", "col"),
            P("dp", "col"),
            P("dp"),
            P("col", "row", None, None, None),
            P("col", "row", None),
            P("col", "row", None),
            P("row", "col", None, None, None),
            P("row", "col", None),
            P("row", "col", None),
        ),
        out_specs=(
            P("dp", "col"),
            P("dp", "col"),
            P("col", "row", "dp", None, None),
            P("row", "col", "dp", None, None),
        ),
        check_vma=False,
    )
```

```python
import jax
import jax.numpy as jnp
from jax import lax
from jax.experimental import pallas as pl
from jax.experimental.pallas import tpu as pltpu
from jax.sharding import PartitionSpec as P

MESH = pl.DeviceIdType.MESH
BF = jnp.bfloat16
F32 = jnp.float32
B = 128
CAP = 256
MB_TOK = 64
COLS = 8
STEPS = 16
TD = 8
NB = 32
LATE, NEAR, FAR = 4, 14, 18
CH = B + 16
QR = 32
HW = 512

NT = (((1,), (1,)), ((), ()))
NN = (((1,), (0,)), ((), ()))


def dot(a, b, dims=NN):
    return lax.dot_general(a, b, dims, preferred_element_type=F32)


def kernel(
    counts, up_rows, up_cols, down_rows, down_cols,
    tokens_in, cotangent_in, up_in, down_in,
    y_out, g_out, gu_out, gd_out,
    tokens, cotangent, up_blocks, down_blocks, inv_v, inv_s, gm, tok_t, gm_t, wup, wdn, part, rbuf, ah, acts, yacc, gacc,
    fs, fr, ys, yr, yo, gbuf, xr, zbuf, zr,
    in_s, inv_sem, rs_s, rs_r, ag_s, ag_r, f_s, f_r, y_s, y_r, ya_s, ya_r, sb_s, sb_r, x_s, x_r, z_s, z_r,
):
    loads = [
        pltpu.make_async_copy(src, dst, in_s.at[i])
        for i, (src, dst) in enumerate(
            ((tokens_in, tokens), (up_in, up_blocks), (cotangent_in, cotangent), (down_in, down_blocks))
        )
    ]
    for load in loads:
        load.start()

    c = lax.axis_index("col")
    row = lax.axis_index("row")
    dp = lax.axis_index("dp")
    core = row % 2
    yi = row // 2
    hi = dp // 4
    xi = dp % 4
    count = counts[0]

    sibling = {"row": row + 1 - 2 * core}
    y_right = {"row": (row + 2) % 8}
    y_left = {"row": (row + 6) % 8}
    x_right = {"dp": hi * 4 + (xi + 1) % 4}
    x_left = {"dp": hi * 4 + (xi + 3) % 4}
    z_right = {"dp": ((hi + 1) % 4) * 4 + xi}
    z_left = {"dp": ((hi + 3) % 4) * 4 + xi}

    def send(src, dst, s_sem, r_sem, device):
        return pltpu.make_async_remote_copy(
            src_ref=src, dst_ref=dst, send_sem=s_sem, recv_sem=r_sem,
            device_id=device, device_id_type=MESH,
        )

    barrier = pltpu.get_barrier_semaphore()
    for peer in (sibling, y_right, y_left, x_right, x_left, z_right, z_left):
        pl.semaphore_signal(barrier, inc=1, device_id=peer, device_id_type=MESH)

    @pl.when(c > 0)
    def _():
        pl.semaphore_signal(barrier, inc=1, device_id={"col": c - 1}, device_id_type=MESH)

    @pl.when(c < 3)
    def _():
        pl.semaphore_signal(barrier, inc=1, device_id={"col": c + 1}, device_id_type=MESH)

    lane = lax.broadcasted_iota(jnp.int32, (8, B), 1)
    for tile, (rows_in, cols_in, wide) in enumerate(((up_rows, up_cols, 16), (down_rows, down_cols, TD))):
        table = jnp.full((8, B), NB, jnp.int32)
        for k in range(NB):
            table = jnp.where(lane == rows_in[k] * wide + cols_in[k], k, table)
        inv_v[tile] = table
    tables = pltpu.make_async_copy(inv_v, inv_s, inv_sem)
    tables.start()

    loads[0].wait()
    loads[1].wait()
    tables.wait()

    inside = jnp.where((c > 0) & (c < 3), 1, 0)
    pl.semaphore_wait(barrier, 8 + inside)

    def place(s):
        q = c + s * (3 - 2 * c)
        return q, c + 1 - 2 * s, c - 1 + 2 * s

    def rs_copy(u, s, device):
        ref = rbuf.at[s * COLS + u % COLS, u // COLS]
        j = s * STEPS + u
        return send(ref, ref, rs_s.at[j], rs_r.at[j], {"col": device})

    def ag_copy(u, s, device):
        ref = ah.at[s * COLS + u % COLS, u // COLS]
        j = s * STEPS + u
        return send(ref, ref, ag_s.at[j], ag_r.at[j], {"col": device})

    def enter(k, kind, both):
        for s in range(2):
            part[k + COLS * s, kind] = both[:, s * B:(s + 1) * B]

        @pl.when(c == 0)
        def _():
            rbuf[k, kind] = both[:, :B].astype(BF)
            rs_copy(k + COLS * kind, 0, 1).start()

        @pl.when(c == 3)
        def _():
            rbuf[k + COLS, kind] = both[:, B:].astype(BF)
            rs_copy(k + COLS * kind, 1, 2).start()

    def hidden_partials(k, carry):
        for s in range(2):
            for i in range(TD):
                iu = inv_s[0, 0, i * 16 + k + COLS * s]
                blk = up_blocks[jnp.minimum(iu, NB - 1)]
                wup[k, i * B:(i + 1) * B, s * B:(s + 1) * B] = jnp.where(iu < NB, blk, jnp.zeros_like(blk))
        enter(k, 0, dot(tokens[...], wup[k]))
        return carry

    def act_partials(k, carry):
        for s in range(2):
            for i in range(TD):
                idn = inv_s[1, 0, (k + COLS * s) * TD + i]
                blk = down_blocks[jnp.minimum(idn, NB - 1)]
                wdn[k, s * B:(s + 1) * B, i * B:(i + 1) * B] = jnp.where(idn < NB, blk, jnp.zeros_like(blk))
        enter(k, 1, dot(gm[...], wdn[k], NT))
        return carry

    lax.fori_loop(0, COLS, hidden_partials, 0)
    live = (lax.broadcasted_iota(jnp.int32, (CAP, 1), 0) // MB_TOK < count).astype(F32)
    loads[2].wait()
    gm[...] = (cotangent[...].astype(F32) * live).astype(BF)
    loads[3].wait()
    lax.fori_loop(0, COLS, act_partials, 0)

    yacc[...] = jnp.zeros_like(yacc)
    gacc[...] = jnp.zeros_like(gacc)
    def transposes(i):
        columns = pl.ds(pl.multiple_of(i * B, B), B)
        tok_t[i] = tokens[:, columns].T
        gm_t[i] = gm[:, columns].T

    first = c // 2

    def sum_step(u, s):
        q, nxt, prv = place(s)
        j = s * COLS + u % COLS
        kind = u // COLS

        @pl.when(q > 0)
        def _():
            rs_copy(u, s, nxt).wait_recv()

        @pl.when((q > 0) & (q < 3))
        def _():
            rbuf[j, kind] = (rbuf[j, kind].astype(F32) + part[j, kind]).astype(BF)
            rs_copy(u, s, nxt).start()

        @pl.when((q == 3) & (kind == 0))
        def _():
            h = rbuf[j, 0].astype(F32) + part[j, 0]
            cdf = 0.5 * (1.0 + lax.erf(h * 0.7071067811865476))
            ah[j, 0] = (h * cdf).astype(BF)
            ag_copy(u, s, prv).start()
            part[j, 0] = cdf + h * jnp.exp(-0.5 * h * h) * 0.3989422804014327

        @pl.when((q == 3) & (kind == 1))
        def _():
            a = rbuf[j, 1].astype(F32) + part[j, 1]
            ah[j, 1] = (a * part[j, 0]).astype(BF)
            ag_copy(u, s, prv).start()

    def share_step(u, s):
        q, nxt, prv = place(s)

        @pl.when(q < 3)
        def _():
            ag_copy(u, s, prv).wait_recv()

        @pl.when((q > 0) & (q < 3))
        def _():
            ag_copy(u, s, prv).start()

    def line(kind):
        def body(it, carry):
            def during(lag, step):
                pl.when((it >= lag) & (it < lag + STEPS))(lambda: step(it - lag))

            if kind == 0:
                during(0, lambda u: sum_step(u, first))
                during(LATE, lambda u: sum_step(u, 1 - first))
                pl.when((it >= COLS) & (it < 2 * COLS))(lambda: transposes(it - COLS))
            during(NEAR, lambda u: share_step(u, 1 - first))

            def last(u):
                share_step(u, first)
                k = u % COLS
                one, two = ah[k, kind], ah[k + COLS, kind]
                both = jnp.concatenate([one, two], axis=1)
                if kind == 0:
                    acts[k] = one
                    acts[k + COLS] = two
                    yacc[...] += dot(both, wdn[k])
                else:
                    gacc[...] += dot(both, wup[k], NT)

            during(FAR, last)
            return carry

        return body

    count_rows = jnp.zeros((16, B), F32) + count.astype(F32)

    order = [(hi + 2) % 4, (hi + 1) % 4, (hi + 3) % 4, hi]
    x1, x2, x3 = (xi + 1) % 4, (xi + 2) % 4, (xi + 3) % 4
    y1, y2, y3 = (yi + 1) % 4, (yi + 2) % 4, (yi + 3) % 4

    def size(arr, b):
        return CH if arr == 1 and b == 0 else B

    def grads(arr, g):
        def body(xq, carry):
            for b in range(2):
                k = (order[g] * 4 + xq) * 2 + b
                if arr == 0:
                    block = dot(gm_t[down_cols[k]], acts[down_rows[k]])
                else:
                    block = dot(tok_t[up_rows[k]], ah[up_cols[k], 1])
                gbuf[arr, g, xq, b, :B, :] = block.astype(BF)
            if arr == 1:
                gbuf[arr, g, xq, 0, B:, :] = count_rows.astype(BF)
            return carry

        lax.fori_loop(0, 4, body, 0)

    def half_of(m):
        return (0, 1, 1, 0, 0, 1)[m]

    def x_msg(arr, g, m):
        b = half_of(m)
        rows = pl.ds(0, size(arr, b))
        place_of = (x2, x2, x1, x3)
        src = gbuf.at[arr, g, place_of[m], b, rows] if m < 4 else xr.at[arr, g, m - 4, rows]
        return send(
            src, xr.at[arr, g, m, rows], x_s.at[arr, g, m], x_r.at[arr, g, m], x_left if m % 2 else x_right
        )

    def x_start(arr, g):
        for m in range(4):
            x_msg(arr, g, m).start()

    def x_relay(arr, g):
        for m in range(2):
            n = size(arr, m)
            x_msg(arr, g, m).wait_recv()
            near = x3 if m else x1
            xr[arr, g, m, :n] = (xr[arr, g, m, :n].astype(F32) + gbuf[arr, g, near, m, :n].astype(F32)).astype(BF)
            x_msg(arr, g, m + 4).start()

    def x_final(arr, g):
        for m in range(2, 6):
            x_msg(arr, g, m).wait_recv()
        for b in range(2):
            n = size(arr, b)
            one, two = (2, 5) if b else (3, 4)
            full = gbuf[arr, g, xi, b, :n].astype(F32) + xr[arr, g, one, :n].astype(F32)
            zbuf[arr, g, b, :n] = (full + xr[arr, g, two, :n].astype(F32)).astype(BF)

    def z_msg(arr, m):
        b = half_of(m)
        rows = pl.ds(0, size(arr, b))
        src = zbuf.at[arr, (0, 0, 1, 2)[m], b, rows] if m < 4 else zr.at[arr, m - 4, rows]
        return send(src, zr.at[arr, m, rows], z_s.at[arr, m], z_r.at[arr, m], z_left if m % 2 else z_right)

    def z_relay(arr, m):
        n = size(arr, m)
        z_msg(arr, m).wait_recv()
        zr[arr, m, :n] = (zr[arr, m, :n].astype(F32) + zbuf[arr, 1 + m, m, :n].astype(F32)).astype(BF)
        z_msg(arr, m + 4).start()

    def z_final(arr, b):
        for m in (2, 5) if b else (3, 4):
            z_msg(arr, m).wait_recv()
        n = size(arr, b)
        one, two = (2, 5) if b else (3, 4)
        return zbuf[arr, 3, b, :n].astype(F32) + zr[arr, one, :n].astype(F32) + zr[arr, two, :n].astype(F32)

    accs = (yacc, gacc)
    mine = pl.multiple_of(core * B, B)
    other = pl.multiple_of((1 - core) * B, B)

    def pair(a):
        return send(fs.at[a], fr.at[a], f_s.at[a], f_r.at[a], sibling)

    def term(a, chunk, half):
        rows = pl.ds(pl.multiple_of(core * B + chunk * QR, QR), QR)
        return accs[a][rows, half * HW:(half + 1) * HW]

    def row_msg(a, m):
        src = ys.at[a, m] if m < 4 else yr.at[a, m - 4]
        return send(src, yr.at[a, m], y_s.at[a, m], y_r.at[a, m], y_left if m % 2 else y_right)

    def share_ref(a, chunk, m):
        return yo.at[core * 4 + chunk, a, half_of(m) if m in (2, 3) else m % 2]

    def share_msg(a, m):
        ref = share_ref(a, (yi, yi, yi, yi, y3, y1)[m], m)
        return send(ref, ref, ya_s.at[a, m], ya_r.at[a, m], y_left if m % 2 else y_right)

    def share_in(a, m):
        ref = share_ref(a, (y3, y1, y3, y1, y2, y2)[m], m)
        return send(ref, ref, ya_s.at[a, m], ya_r.at[a, m], y_left if m % 2 else y_right)

    def twin(a, m, half):
        ref = yo.at[half * 4 + (yi, y3, y1, y2)[m], a]
        return send(ref, ref, sb_s.at[a, m], sb_r.at[a, m], sibling)

    def row_pair(a):
        fs[a] = accs[a][pl.ds(other, B), :].astype(BF)
        pair(a).start()

    def row_start(a):
        pair(a).wait_recv()
        accs[a][pl.ds(mine, B), :] += fr[a].astype(F32)
        for m in range(4):
            ys[a, m] = term(a, (y2, y2, y1, y3)[m], half_of(m)).astype(BF)
            row_msg(a, m).start()

    def row_relay(a):
        for m in range(2):
            row_msg(a, m).wait_recv()
            yr[a, m] = (yr[a, m].astype(F32) + term(a, (y1, y3)[m], m)).astype(BF)
            row_msg(a, m + 4).start()

    def row_final(a):
        for m in range(2, 6):
            row_msg(a, m).wait_recv()
        for b in range(2):
            one, two = (2, 5) if b else (3, 4)
            full = term(a, yi, b) + yr[a, one].astype(F32) + yr[a, two].astype(F32)
            if a == 0:
                full = full * (core * 2 + yi // 2 < count).astype(F32)
            yo[core * 4 + yi, a, b] = full.astype(BF)
        for m in range(4):
            share_msg(a, m).start()
        twin(a, 0, core).start()

    def row_pass(a):
        for m in range(2):
            share_in(a, m).wait_recv()
            share_msg(a, m + 4).start()
        for m in range(2):
            share_in(a, m + 2).wait_recv()
            twin(a, m + 1, core).start()

    def row_end(a):
        share_in(a, 4).wait_recv()
        share_in(a, 5).wait_recv()
        twin(a, 3, core).start()

    def row_out(a, out):
        for m in range(4):
            twin(a, m, 1 - core).wait_recv()
        for chunk in range(8):
            for b in range(2):
                out[chunk * QR:(chunk + 1) * QR, b * HW:(b + 1) * HW] = yo[chunk, a, b]

    after = FAR + COLS
    lax.fori_loop(0, after, line(0), 0)

    def on(first_step, steps):
        lax.fori_loop(after + first_step, after + first_step + steps, line(1), 0)

    row_pair(0)
    grads(0, 0)
    x_start(0, 0)
    grads(0, 1)
    x_start(0, 1)
    on(0, 1)
    grads(0, 2)
    x_start(0, 2)
    grads(0, 3)
    x_start(0, 3)
    on(1, 1)
    row_start(0)
    x_relay(0, 0)
    on(2, 2)
    x_relay(0, 1)
    row_relay(0)
    on(4, 1)
    x_relay(0, 2)
    x_relay(0, 3)
    on(5, 1)
    row_final(0)
    on(6, 2)

    row_pair(1)
    grads(1, 0)
    x_start(1, 0)
    x_final(0, 0)
    z_msg(0, 0).start()
    z_msg(0, 1).start()
    x_final(0, 1)
    z_msg(0, 2).start()
    x_final(0, 2)
    z_msg(0, 3).start()
    grads(1, 1)
    x_start(1, 1)
    row_start(1)
    x_relay(1, 0)
    grads(1, 2)
    x_start(1, 2)
    z_relay(0, 0)
    z_relay(0, 1)
    x_relay(1, 1)
    row_relay(1)
    grads(1, 3)
    x_start(1, 3)
    x_final(1, 0)
    z_msg(1, 0).start()
    z_msg(1, 1).start()
    x_relay(1, 2)
    row_pass(0)
    row_final(1)
    x_final(1, 1)
    z_msg(1, 2).start()
    x_relay(1, 3)
    x_final(1, 2)
    z_msg(1, 3).start()
    row_end(0)
    row_pass(1)
    x_final(0, 3)
    x_final(1, 3)
    row_out(0, y_out)
    down0 = z_final(0, 0)
    down1 = z_final(0, 1)
    z_relay(1, 0)
    z_relay(1, 1)
    row_end(1)
    row_out(1, g_out)

    up0 = z_final(1, 0)
    total = up0[B:B + 1, :]
    gu_out[0] = up0[:B, :] / total
    gd_out[0] = (down0 / total).T
    gd_out[1] = (down1 / total).T
    gu_out[1] = z_final(1, 1) / total

    for s in range(2):
        q, nxt, prv = place(s)

        @pl.when(q < 3)
        def _(s=s, nxt=nxt):
            lax.fori_loop(0, STEPS, lambda u, v: (rs_copy(u, s, nxt).wait_send(), v)[1], 0)

        @pl.when(q > 0)
        def _(s=s, prv=prv):
            lax.fori_loop(0, STEPS, lambda u, v: (ag_copy(u, s, prv).wait_send(), v)[1], 0)

    for arr in range(2):
        pair(arr).wait_send()
        for m in range(6):
            row_msg(arr, m).wait_send()
            share_msg(arr, m).wait_send()
            z_msg(arr, m).wait_send()
            for g in range(4):
                x_msg(arr, g, m).wait_send()
        for m in range(4):
            twin(arr, m, core).wait_send()


def store(y, g, u, d, y_to, g_to, u_to, d_to, y_v, g_v, u_v, d_v, in_sem, out_sem):
    arrays = ((y, y_v, y_to), (g, g_v, g_to), (u, u_v, u_to), (d, d_v, d_to))
    into = [pltpu.make_async_copy(src, mid, in_sem.at[i]) for i, (src, mid, dst) in enumerate(arrays)]
    out = [pltpu.make_async_copy(mid, dst, out_sem.at[i]) for i, (src, mid, dst) in enumerate(arrays)]
    for copy in into:
        copy.start()
    for i in range(4):
        into[i].wait()
        out[i].start()
    for copy in out:
        copy.wait()


def body(tokens, cotangent, counts, up_blocks, up_rows, up_cols, down_blocks, down_rows, down_cols):
    ur, uc = up_rows[0, 0], up_cols[0, 0]
    dr, dc = down_rows[0, 0], down_cols[0, 0]
    smem = pl.BlockSpec(memory_space=pltpu.SMEM)
    vmem = pl.BlockSpec(memory_space=pltpu.VMEM)
    hbm = pl.BlockSpec(memory_space=pltpu.HBM)
    width = TD * B
    dma = pltpu.SemaphoreType.DMA
    shapes = (
        jax.ShapeDtypeStruct((CAP, width), BF),
        jax.ShapeDtypeStruct((CAP, width), BF),
        jax.ShapeDtypeStruct((2, B, B), F32),
        jax.ShapeDtypeStruct((2, B, B), F32),
    )
    results = pl.pallas_call(
        kernel,
        out_shape=shapes,
        in_specs=[smem] * 5 + [hbm] * 4,
        out_specs=(vmem,) * 4,
        scratch_shapes=[
            pltpu.VMEM((CAP, width), BF),
            pltpu.VMEM((CAP, width), BF),
            pltpu.VMEM((NB, B, B), BF),
            pltpu.VMEM((NB, B, B), BF),
            pltpu.VMEM((2, 8, B), jnp.int32),
            pltpu.SMEM((2, 8, B), jnp.int32),
            pltpu.VMEM((CAP, width), BF),
            pltpu.VMEM((TD, B, CAP), BF),
            pltpu.VMEM((TD, B, CAP), BF),
            pltpu.VMEM((STEPS, width, 2 * B), BF),
            pltpu.VMEM((STEPS, 2 * B, width), BF),
            pltpu.VMEM((16, 2, CAP, B), F32),
            pltpu.VMEM((16, 2, CAP, B), BF),
            pltpu.VMEM((16, 2, CAP, B), BF),
            pltpu.VMEM((16, CAP, B), BF),
            pltpu.VMEM((CAP, width), F32),
            pltpu.VMEM((CAP, width), F32),
            pltpu.VMEM((2, B, width), BF),
            pltpu.VMEM((2, B, width), BF),
            pltpu.VMEM((2, 4, QR, HW), BF),
            pltpu.VMEM((2, 6, QR, HW), BF),
            pltpu.VMEM((8, 2, 2, QR, HW), BF),
            pltpu.VMEM((2, 4, 4, 2, CH, B), BF),
            pltpu.VMEM((2, 4, 6, CH, B), BF),
            pltpu.VMEM((2, 4, 2, CH, B), BF),
            pltpu.VMEM((2, 6, CH, B), BF),
            dma((4,)), dma, dma((32,)), dma((32,)), dma((32,)), dma((32,)),
            dma((2,)), dma((2,)), dma((2, 6)), dma((2, 6)), dma((2, 6)), dma((2, 6)), dma((2, 4)), dma((2, 4)),
            dma((2, 4, 6)), dma((2, 4, 6)), dma((2, 6)), dma((2, 6)),
        ],
        compiler_params=pltpu.CompilerParams(
            collective_id=0, has_side_effects=True, vmem_limit_bytes=56 << 20
        ),
    )(counts, ur, uc, dr, dc, tokens, cotangent, up_blocks[0, 0], down_blocks[0, 0])
    y_out, g_out, gu, gd = pl.pallas_call(
        store,
        out_shape=shapes,
        in_specs=[hbm] * 4,
        out_specs=(hbm,) * 4,
        scratch_shapes=[pltpu.VMEM(shape.shape, shape.dtype) for shape in shapes] + [dma((4,)), dma((4,))],
    )(*results)
    return y_out, g_out, gu[None, None], gd[None, None]


def solution(mesh):
    return jax.shard_map(
        body,
        mesh=mesh,
        in_specs=(
            P("dp", "col"),
            P("dp", "col"),
            P("dp"),
            P("col", "row", None, None, None),
            P("col", "row", None),
            P("col", "row", None),
            P("row", "col", None, None, None),
            P("row", "col", None),
            P("row", "col", None),
        ),
        out_specs=(
            P("dp", "col"),
            P("dp", "col"),
            P("col", "row", "dp", None, None),
            P("row", "col", "dp", None, None),
        ),
        check_vma=False,
    )
```
